32 devices in a mesh: scene: 2 (over x), az: 8 (over z, y), rg: 2 (over core).
Axes of the slice: x: 2, y: 2, z: 4, core: 2. Of those that a mesh axis runs over, the one named last changes fastest.
Arguments:
- complex_phase_image: float32 [2, 1024, 1024], P(None, ('scene', 'az'), 'rg'), parts along dimension 1, may hold values from -6 to 6
- phase_to_topography_factor: float32 [1024, 1024], P(('scene', 'az'), 'rg'), parts along dimension 0, may hold values from 0.5 to 3
- terrain_model_heights: float32 [128, 16, 1024], P(('scene', 'az'), 'rg'), parts along dimension 0, may hold values from -6 to 6
- radar_parcel_listing: int32 [32, 9], P(('scene', 'az', 'rg')), parts along dimension 0, may hold values from -1 to 1023, as said below
- pixel_terrain_position: int32 [1024, 1024], P(('scene', 'az'), 'rg'), parts along dimension 0, may hold values from 0 to 9215, as said below
- multilook_receiving_patch: int32 [65536, 1], P(('scene', 'az', 'rg')), parts along dimension 0, may hold values from 0 to 15; in each aligned block of 2048 rows (0 to 2047, 2048 to 4095, ...) at most 256 rows name the same one
- multilook_base_point: int32 [65536], P(('scene', 'az', 'rg')), parts along dimension 0, may hold values from 0 to 2047
- multilook_splat_shares: float32 [4, 65536], P(None, ('scene', 'az', 'rg')), parts along dimension 1, may hold values from 0 to 1
Outputs:
- geocoded: float32 [2, 256, 256], P(None, ('scene', 'az'), 'rg'), parts along dimension 1
The draws below stay inside these ranges and needn't reach their ends.
There are 2 independent parts, one for each index of `scene`. The reference program is written for one: setup_inputs(seed, part) draws one part's arguments, and reference() takes and returns one part's arrays. A program takes and returns all parts, laid end to end along the dimension named above; each array names one. Nothing has to cross between parts.
Inputs may be any that keep to these rules, and one draw needn't show every extreme that they name: `radar_parcel_listing`: entries are sub-block numbers lat * 16 + lon; each tile lists a rectangle of at most 3 x 3 sub-blocks in row-major order, then -1 padding. Tile (a, r) lists only sub-blocks with c * 8 - 1 <= lat <= (c + 1) * 8 for one map latitude row c (any row, not tied to a) and r * 8 - 1 <= lon <= (r + 1) * 8. Some tile has exactly 9 listed blocks. pixel_terrain_position // 1024 is a listed, non-padding slot of the pixel's own tile. `multilook_receiving_patch`: among the rows of one device (aligned blocks of 2048 rows) at most 256 name one map tile; some map tile is named by exactly 256 rows of some device.
All inputs are finite; a program needn't handle non-finite values.
Results may differ from the reference program's by a relative error of at most 0.00015.
Values sent between devices are 32-bit elements; how exact they have to be, the bound alone decides.
No kernel may reach another device: no remote copies, remote signals or barrier semaphores. Data moves between devices by JAX's collectives and lax.ppermute only.
A program may use at most 64 MiB of HBM per device.

```python
import math
import jax
import jax.numpy as jnp
import numpy as np
from jax import lax

AZIMUTH_PER_TILE = 64
RANGE_PER_TILE = 512
PATCH = 64
LOOK = 4
SB_A = 8
SB_R = 8
PARCEL_SAMPLES = 1024
FOOTPRINT_SLOTS = 9
TILE_COUNT = 16
ML = 16
MW = 128
LOOKS_DEV = 2048
CAP = 256
RAZ = 512
RRG = 1024
NORTHWARD_PARTS = 64
EASTWARD_PARTS = 16
MLAT = 128
MLON = 256
N_AZ = 8
N_RG = 2


def footprint_table(key):
    keys = jax.random.split(jax.random.fold_in(key, 11), 6)
    tile_ids = jnp.arange(TILE_COUNT, dtype=jnp.int32)
    tile_az = tile_ids // N_RG
    tile_rg = tile_ids % N_RG
    forced = jax.random.randint(keys[0], (), 0, TILE_COUNT)
    is_forced = tile_ids == forced
    row_shift = jax.random.randint(keys[5], (TILE_COUNT,), 0, N_AZ)
    row_shift = jnp.where(is_forced, N_AZ // 2, row_shift)
    target_az = (tile_az + row_shift) % N_AZ
    height_blocks = jnp.where(is_forced, 3, jax.random.randint(keys[1], (TILE_COUNT,), 1, 4))
    width_blocks = jnp.where(is_forced, 3, jax.random.randint(keys[2], (TILE_COUNT,), 1, 4))
    lat_low = jnp.maximum(target_az * SB_A - 1, 0)
    lat_high = jnp.minimum((target_az + 1) * SB_A, NORTHWARD_PARTS - 1) - height_blocks + 2
    lon_low = jnp.maximum(tile_rg * SB_R - 1, 0)
    lon_high = jnp.minimum((tile_rg + 1) * SB_R, EASTWARD_PARTS - 1) - width_blocks + 2
    lat_start = jax.random.randint(keys[3], (TILE_COUNT,), lat_low, lat_high)
    lon_start = jax.random.randint(keys[4], (TILE_COUNT,), lon_low, lon_high)
    lat_start = jnp.where(is_forced, jnp.minimum(target_az * SB_A, NORTHWARD_PARTS - 3), lat_start)
    lon_start = jnp.where(is_forced, jnp.minimum(tile_rg * SB_R, EASTWARD_PARTS - 3), lon_start)
    slot_ids = jnp.arange(FOOTPRINT_SLOTS, dtype=jnp.int32)[None, :]
    down_step = slot_ids // width_blocks[:, None]
    side_step = slot_ids % width_blocks[:, None]
    inside = slot_ids < (height_blocks * width_blocks)[:, None]
    numbers = (lat_start[:, None] + down_step) * EASTWARD_PARTS + lon_start[:, None] + side_step
    table_out = jnp.where(inside, numbers, -1).astype(jnp.int32)
    return (table_out, (height_blocks * width_blocks).astype(jnp.int32))


def draw_radar_parcel_listing(key, part):
    return footprint_table(key)[0]


def draw_pixel_terrain_position(key, part):
    listed = footprint_table(key)[1]
    pixel_rows = jnp.arange(RAZ, dtype=jnp.int32) // AZIMUTH_PER_TILE
    pixel_cols = jnp.arange(RRG, dtype=jnp.int32) // RANGE_PER_TILE
    pixel_tile = pixel_rows[:, None] * N_RG + pixel_cols[None, :]
    limit = listed[pixel_tile] * PARCEL_SAMPLES
    return jax.random.randint(jax.random.fold_in(key, 23), (RAZ, RRG), 0, limit).astype(jnp.int32)


def with_ends(result, rng, least, top_value):
    index_at = [jax.random.randint(jax.random.fold_in(rng, axis), (), 0, length) for axis, length in enumerate(result.shape)]
    longest = result.shape.index(max(result.shape))
    beside = index_at[:longest] + [(index_at[longest] + 1) % result.shape[longest]] + index_at[longest + 1:]
    return result.at[tuple(index_at)].set(least).at[tuple(beside)].set(top_value)


def block_scale(stream_key, dims, cuts, least, high):
    factor_of = 1.0
    for dim, shards_of in cuts:
        steps = jax.random.uniform(jax.random.fold_in(jax.random.fold_in(stream_key, 6), dim), (shards_of,), jnp.float32, least / len(cuts), high / len(cuts))
        factor_of = factor_of * jnp.repeat(jnp.exp(steps), dims[dim] // shards_of).reshape((-1,) + (1,) * (len(dims) - 1 - dim))
    return factor_of


def deal_out(stream_key, own, number, rows, count, top, most, skew):
    order = jax.random.permutation(stream_key, count)
    crowded, ordinary = load_shares(count, rows * top, most, skew, True), load_shares(count, rows * top, most, skew, False)
    places = jnp.arange(count)

    def named(sizes, turn):
        used = int((sizes > 0).sum())
        fixed = max(1, used // 4)
        moved = fixed + (places - fixed + turn * (used - fixed)) % max(1, count - fixed)
        return jnp.zeros((count,), jnp.int32).at[order[jnp.where(places < fixed, places, moved)]].set(jnp.asarray(sizes, jnp.int32))

    sizes = jnp.where(number % 4 == 0, named(crowded, number // 4), named(ordinary, number - number // 4 - 1))
    mixed = jax.random.permutation(jax.random.fold_in(own, 3), count)
    giver, sink = mixed[0:count // 2 * 2:2], mixed[1:count // 2 * 2:2]
    margin = jnp.minimum(sizes[giver] - 1, most - sizes[sink]) // 2
    margin = jnp.where((giver == order[0]) | (sink == order[0]) | (sizes[sink] == 0), 0, jnp.maximum(margin, 0))
    moved = jax.random.randint(jax.random.fold_in(own, 4), (count // 2,), 0, 1 << 20) % (margin + 1)
    sizes = sizes.at[giver].add(-moved).at[sink].add(moved)
    labels = jnp.searchsorted(jnp.cumsum(sizes), jnp.arange(rows * top), side="right").astype(jnp.int32)
    grid = labels.reshape(top, rows).T
    grid = grid[jax.random.permutation(jax.random.fold_in(own, 1), rows)]
    turn = jax.random.randint(jax.random.fold_in(own, 2), (rows, 1), 0, top)
    return jnp.take_along_axis(grid, (jnp.arange(top)[None, :] + turn) % top, axis=1)


def load_shares(count, total, bound, skew, full):
    portions = [(1 << 20) // math.isqrt(rank ** skew) + 1 for rank in range(1, count + 1)]
    largest = bound if full else min(bound, max(-(-total // count), total * portions[0] // sum(portions)))
    least = 1 if total - largest >= count - 1 else 0
    given, surplus = [largest] + [least] * (count - 1), total - largest - least * (count - 1)
    while surplus > 0:
        candidates = [i for i in range(1, count) if given[i] < largest] or [i for i in range(1, count) if given[i] < bound]
        whole, budget = sum([portions[i] for i in candidates]), surplus
        for i in candidates:
            extra = min(bound - given[i], max(1, budget * portions[i] // whole), surplus)
            given[i] = given[i] + extra
            surplus = surplus - extra
    return np.array(given)


def centred(own_key, extent, deviation, reach, cuts=(), held_as=jnp.bfloat16):
    level = block_scale(own_key, extent, cuts, -0.22, 0.18) if cuts else 1.0
    values = jax.random.normal(own_key, extent, jnp.float32) * deviation * level
    return jnp.minimum(jnp.maximum(values, -reach), reach).astype(held_as)


def setup_inputs(seed: int = 0, part: int = 0) -> dict:
    splits = jax.random.split(jax.random.key(seed), 9)
    part_keys = jax.random.split(jax.random.fold_in(splits[8], part), 9)
    complex_phase_image = centred(part_keys[0], (2, RAZ, RRG), 1.0, 6.0, ((1, 8), (2, 2)), jnp.float32)
    phase_to_topography_factor = jnp.clip(0.5 + 2.5 * jax.random.uniform(part_keys[1], (RAZ, RRG), jnp.float32) ** block_scale(part_keys[1], (RAZ, RRG), ((0, 8), (1, 2)), -0.2, 0.2), 0.5, 3.0)
    terrain_model_heights = centred(part_keys[2], (NORTHWARD_PARTS, EASTWARD_PARTS, PARCEL_SAMPLES), 1.0, 6.0, ((0, 8), (1, 2)), jnp.float32)
    radar_parcel_listing = draw_radar_parcel_listing(jax.random.fold_in(jax.random.fold_in(splits[8], part), 71), part)
    pixel_terrain_position = draw_pixel_terrain_position(jax.random.fold_in(jax.random.fold_in(splits[8], part), 71), part)
    multilook_receiving_patch_keys = jax.random.split(jax.random.fold_in(part_keys[5], 1), (TILE_COUNT * LOOKS_DEV) // LOOKS_DEV)
    multilook_receiving_patch_turns = jax.random.permutation(jax.random.fold_in(part_keys[5], 3), (TILE_COUNT * LOOKS_DEV) // LOOKS_DEV)
    multilook_receiving_patch = jax.vmap(lambda own, number: deal_out(jax.random.fold_in(part_keys[5], 2), own, number, LOOKS_DEV, TILE_COUNT, 1, CAP, 2))(multilook_receiving_patch_keys, multilook_receiving_patch_turns).reshape((TILE_COUNT * LOOKS_DEV, 1))
    multilook_base_point = with_ends(jax.random.randint(part_keys[6], (TILE_COUNT * LOOKS_DEV,), 0, ML * MW), jax.random.fold_in(part_keys[6], 1), 0, (ML * MW) - 1).astype(jnp.int32)
    multilook_splat_shares = jnp.clip(1.0 * jax.random.uniform(part_keys[7], (4, TILE_COUNT * LOOKS_DEV), jnp.float32) ** block_scale(part_keys[7], (4, TILE_COUNT * LOOKS_DEV), ((1, 16),), -0.2, 0.2), 0.0, 1.0)
    return {"complex_phase_image": complex_phase_image, "phase_to_topography_factor": phase_to_topography_factor, "terrain_model_heights": terrain_model_heights, "radar_parcel_listing": radar_parcel_listing, "pixel_terrain_position": pixel_terrain_position, "multilook_receiving_patch": multilook_receiving_patch, "multilook_base_point": multilook_base_point, "multilook_splat_shares": multilook_splat_shares}


EPS = 1e-06

def box_mean(magnitude):
    summed = jnp.zeros_like(magnitude)
    for shift_a in (-1, 0, 1):
        for shift_b in (-1, 0, 1):
            summed = summed + jnp.roll(jnp.roll(magnitude, shift_a, axis=1), shift_b, axis=2)
    return summed / 9.0

def reference(complex_phase_image, phase_to_topography_factor, terrain_model_heights, radar_parcel_listing, pixel_terrain_position, multilook_receiving_patch, multilook_base_point, multilook_splat_shares):
    terrain_raveled = terrain_model_heights.reshape(NORTHWARD_PARTS * EASTWARD_PARTS, PARCEL_SAMPLES)
    block_grid = terrain_raveled[jnp.maximum(radar_parcel_listing, 0)].reshape(TILE_COUNT, FOOTPRINT_SLOTS * PARCEL_SAMPLES)
    index_of_tile = pixel_terrain_position.reshape(N_AZ, AZIMUTH_PER_TILE, N_RG, RANGE_PER_TILE).transpose(0, 2, 1, 3).reshape(TILE_COUNT, AZIMUTH_PER_TILE * RANGE_PER_TILE)
    height_values = jnp.take_along_axis(block_grid, index_of_tile, axis=1)
    height_values = height_values.reshape(N_AZ, N_RG, AZIMUTH_PER_TILE, RANGE_PER_TILE).transpose(0, 2, 1, 3).reshape(RAZ, RRG)
    topo_phase = phase_to_topography_factor * height_values
    cosine_phase = jnp.cos(topo_phase)
    sine_phase = jnp.sin(topo_phase)
    real_part = complex_phase_image[0] * cosine_phase + complex_phase_image[1] * sine_phase
    imag_part = complex_phase_image[1] * cosine_phase - complex_phase_image[0] * sine_phase
    rim = PATCH // 4
    step = PATCH // 2
    padded = jnp.pad(jnp.stack([real_part, imag_part]), ((0, 0), (rim, rim), (rim, rim)))
    block_cols = RRG // step

    def filter_row(strip_index):
        strip = lax.dynamic_slice_in_dim(padded, strip_index * step, PATCH, axis=1)
        pieces = strip.reshape(2, PATCH, block_cols + 1, step)
        pairs = jnp.concatenate([pieces[:, :, :-1], pieces[:, :, 1:]], axis=3)
        complex_field = (pairs[0] + 1j * pairs[1]).transpose(1, 0, 2)
        spectrum = jnp.fft.fft2(complex_field)
        smooth = box_mean(jnp.abs(spectrum))
        spectral_gain = jnp.sqrt(smooth / (lax.optimization_barrier(jnp.mean(smooth, axis=(1, 2), keepdims=True)) + EPS))
        restored = jnp.fft.ifft2(spectrum * spectral_gain)[:, rim:rim + step, rim:rim + step]
        core_cells = restored.transpose(1, 0, 2).reshape(step, block_cols * step)
        return jnp.stack([jnp.real(core_cells), jnp.imag(core_cells)])
    strips = lax.map(filter_row, jnp.arange(RAZ // step, dtype=jnp.int32))
    filtered = strips.transpose(1, 0, 2, 3).reshape(2, RAZ, RRG)
    looks = filtered.reshape(2, RAZ // LOOK, LOOK, RRG // LOOK, LOOK).mean(axis=(2, 4))
    looks = looks.reshape(2, N_AZ, ML, N_RG, MW).transpose(0, 1, 3, 2, 4).reshape(2, TILE_COUNT * LOOKS_DEV)
    owner_tile = multilook_receiving_patch[:, 0]
    lat_cell = owner_tile // N_RG * ML + multilook_base_point // MW
    lon_cell = owner_tile % N_RG * MW + multilook_base_point % MW
    stride = MLON + 1
    base = lat_cell * stride + lon_cell
    corners = jnp.concatenate([base, base + 1, base + stride, base + stride + 1])
    weights = multilook_splat_shares.reshape(-1)
    contributions = jnp.stack([jnp.tile(looks[0], 4) * weights, jnp.tile(looks[1], 4) * weights, weights])
    accumulated = jnp.zeros((3, (MLAT + 1) * stride), dtype=jnp.float32).at[:, corners].add(contributions)
    grid_sums = accumulated.reshape(3, MLAT + 1, stride)[:, :MLAT, :MLON]
    return grid_sums[:2] / jnp.maximum(grid_sums[2:3], 1.0)
```

```python
import functools
import math

import jax
import jax.numpy as jnp
import numpy as np
from jax import lax
from jax.experimental import pallas as pl
from jax.experimental.pallas import tpu as pltpu
from jax.sharding import PartitionSpec as P

PATCH = 64
LOOK = 4
EPS = 1e-06
LANES = 128
RIM = PATCH // 4
STEP = PATCH // 2
HALF = PATCH // 2
F32 = jnp.float32
BF16 = jnp.bfloat16
I32 = jnp.int32
VMEM = pltpu.VMEM
VSPEC = pl.BlockSpec(memory_space=pltpu.VMEM)
SSPEC = pl.BlockSpec(memory_space=pltpu.SMEM)


def call(kernel, outs, args, scratch=(), smem=(), cost=(1_000_000, 1_000_000)):
    return pl.pallas_call(
        kernel,
        out_shape=outs,
        in_specs=[SSPEC if i in smem else VSPEC for i in range(len(args))],
        out_specs=jax.tree.map(lambda _: VSPEC, outs),
        scratch_shapes=list(scratch),
        cost_estimate=pl.CostEstimate(flops=cost[0], bytes_accessed=cost[1], transcendentals=0),
    )(*args)


def sds(shape, dtype=F32):
    return jax.ShapeDtypeStruct(shape, dtype)


def split(x):
    hi = x.astype(BF16)
    return hi, (x - hi.astype(F32)).astype(BF16)


def dot(a, b):
    return jnp.dot(a, b, preferred_element_type=F32)


def dot_nt(a, b):
    return lax.dot_general(a, b, (((1,), (1,)), ((), ())), preferred_element_type=F32)


def lane_iota(shape):
    return lax.broadcasted_iota(I32, shape, len(shape) - 1)


def row_iota(shape):
    return lax.broadcasted_iota(I32, shape, 0)


def roll(x, shift, axis):
    shift = shift % x.shape[axis]
    return x if shift == 0 else pltpu.roll(x, shift, axis)


def lane_gather(row, index):
    return jnp.take_along_axis(jnp.broadcast_to(row, index.shape), index, axis=1)


def host_split(x):
    hi = np.asarray(x, np.float32).astype(BF16)
    lo = (np.asarray(x, np.float64) - hi.astype(np.float64)).astype(BF16)
    return hi, lo


def filter_tables(block_rows):
    turn = 2.0 * math.pi / PATCH
    step = np.arange(PATCH)
    cosine = np.cos(turn * (step[:, None] * step[None, :] % PATCH))
    sine = np.sin(turn * (step[:, None] * step[None, :] % PATCH))
    rows = block_rows * STEP + 2 * RIM
    count = block_rows * PATCH
    az = np.zeros((2 * count, 2 * rows))
    for u in range(block_rows):
        k = slice(u * PATCH, (u + 1) * PATCH)
        ki = slice(count + u * PATCH, count + (u + 1) * PATCH)
        h = slice(u * STEP, u * STEP + PATCH)
        hi = slice(rows + u * STEP, rows + u * STEP + PATCH)
        az[k, h], az[k, hi] = cosine, sine
        az[ki, h], az[ki, hi] = -sine, cosine
    pieces = LANES // HALF
    rg = np.zeros((2 * LANES, pieces * 2 * PATCH))
    for q in range(pieces):
        w = slice(q * HALF, (q + 1) * HALF)
        wi = slice(LANES + q * HALF, LANES + (q + 1) * HALF)
        lr = slice(q * 2 * PATCH, q * 2 * PATCH + PATCH)
        li = slice(q * 2 * PATCH + PATCH, (q + 1) * 2 * PATCH)
        rg[w, lr], rg[wi, lr] = cosine[:HALF], sine[:HALF]
        rg[w, li], rg[wi, li] = -sine[:HALF], cosine[:HALF]
    looks = STEP // LOOK
    core = cosine[RIM : RIM + STEP].reshape(looks, LOOK, PATCH).mean(axis=1)
    core_s = sine[RIM : RIM + STEP].reshape(looks, LOOK, PATCH).mean(axis=1)
    back = np.zeros((2 * block_rows * looks, count))
    for u in range(block_rows):
        k = slice(u * PATCH, (u + 1) * PATCH)
        back[u * looks : (u + 1) * looks, k] = core / PATCH
        back[(block_rows + u) * looks : (block_rows + u + 1) * looks, k] = core_s / PATCH
    c_l, s_l = core.T / PATCH, core_s.T / PATCH
    reps = LANES // looks
    last = np.concatenate(
        [
            np.concatenate([np.tile(c_l, reps), np.tile(s_l, reps)], axis=1),
            np.concatenate([np.tile(-s_l, reps), np.tile(c_l, reps)], axis=1),
            np.concatenate([np.tile(-s_l, reps), np.tile(c_l, reps)], axis=1),
            np.concatenate([np.tile(-c_l, reps), np.tile(-s_l, reps)], axis=1),
        ],
        axis=0,
    )
    return az, rg, back, last


def slice_kernel(width, dem_ref, list_ref, out_ref):
    tiles = out_ref.shape[0]
    lats, lons, _ = dem_ref.shape
    packed = LANES // width
    groups = lats // packed
    slots = list_ref.shape[1]
    lane = lane_iota((lons, LANES))
    listed = list_ref[...].astype(F32)
    for q in range(tiles):
        tile, offset = divmod(q * width, LANES)
        for g in range(groups):
            total = None
            for p in range(packed):
                x = dem_ref[p * groups + g, :, tile * LANES : (tile + 1) * LANES]
                x = roll(x, p * width - offset, 1)
                total = x if total is None else jnp.where(lane // width == p, x, total)
            out_ref[q, g * lons : (g + 1) * lons, :] = total
        out_ref[q, groups * lons : groups * lons + 1, 0:slots] = listed


def halo_kernel(par_ref, image_ref, factor_ref, position_ref, one_ref, two_ref):
    even = par_ref[0] == 0
    lines = factor_ref.shape[0]
    fields = (
        lambda s: image_ref[0, s, :],
        lambda s: image_ref[1, s, :],
        lambda s: factor_ref[s, :],
        lambda s: position_ref[s, :].astype(F32),
    )
    for i, field in enumerate(fields):
        first = field(slice(0, RIM))
        last = field(slice(lines - RIM, lines))
        one_ref[i] = jnp.where(even, last, first)
        two_ref[i] = jnp.where(even, first, last)


def border_rows(b0, b1, n_rg):
    tiles = b0.shape[0]
    dest = row_iota(b0.shape)
    shifted = roll(b1, 1, 1)
    below = roll(b0, n_rg, 0)
    beside = roll(shifted, n_rg, 0)
    diagonal = jnp.where(dest % n_rg > 0, roll(shifted, n_rg + 1, 0), 0.0)
    beside = jnp.where(lane_iota(b0.shape) == 0, diagonal, beside)
    return jnp.where(dest >= n_rg, below + beside, 0.0)


def pack_kernel(n_rg, cap_rows, owner_ref, base_ref, share_ref, early_ref, im_ref, in_ref, mask_ref, col_ref, hot_ref, lhs_ref):
    tiles = early_ref.shape[0]
    height, width = owner_ref.shape
    owner = owner_ref[...]
    batch = min(tiles, 16)
    tri = (row_iota((width, width)) < lane_iota((width, width))).astype(BF16)
    ones = jnp.ones((width, width), BF16)
    size = batch * height
    r, c = row_iota((size, size)), lane_iota((size, size))
    lower = ((r // height == c // height) & (c < r)).astype(BF16)
    rank = jnp.zeros((height, width), F32)
    for b in range(tiles // batch):
        hot = jnp.concatenate([(owner == b * batch + o).astype(F32) for o in range(batch)], axis=0)
        hot16 = hot.astype(BF16)
        before = dot(hot16, tri) + dot(lower, dot(hot16, ones).astype(BF16))
        kept = hot * before
        for o in range(batch):
            rank = rank + kept[o * height : (o + 1) * height]
    rank = rank.astype(I32)
    base = base_ref[...]
    column = base % width
    line = base // width
    cap = cap_rows * LANES
    for m in range(height):
        cut = slice(m * width, (m + 1) * width)
        hot_ref[:, cut] = (row_iota((cap, width)) == rank[m : m + 1]).astype(F32).astype(BF16)
        col_ref[:, cut] = (row_iota((width, width)) == column[m : m + 1]).astype(F32).astype(BF16)
        mine = row_iota((tiles, width)) == owner[m : m + 1]
        lhs_ref[0:tiles, cut] = mine.astype(F32).astype(BF16)
        lhs_ref[tiles : 2 * tiles, cut] = jnp.where(mine, float(m), 0.0).astype(BF16)
        lhs_ref[2 * tiles :, cut] = jnp.where(mine, lane_iota((tiles, width)).astype(F32), 0.0).astype(BF16)
        edge = mine & (line[m : m + 1] == height - 1)
        mask_ref[0:tiles, cut] = jnp.where(edge, share_ref[2, m : m + 1, :], 0.0)
        mask_ref[tiles:, cut] = jnp.where(edge, share_ref[3, m : m + 1, :], 0.0)
    found = dot_nt(lhs_ref[...], hot_ref[...])
    valid = found[0:tiles] > 0.5
    at_m = found[tiles : 2 * tiles].astype(I32)
    at_n = found[2 * tiles :].astype(I32)
    im_ref[...] = at_m
    in_ref[...] = at_n
    cell = base.astype(F32)
    for channel in range(5):
        for k in range(cap_rows):
            cut = slice(k * LANES, (k + 1) * LANES)
            total = jnp.zeros((tiles, LANES), F32)
            for m in range(height):
                row = cell[m : m + 1] if channel == 4 else share_ref[channel, m : m + 1, :]
                total = jnp.where(at_m[:, cut] == m, lane_gather(row, at_n[:, cut]), total)
            early_ref[:, channel * cap_rows + k, :] = jnp.where(valid[:, cut], total, 0.0)
    high, low = split(mask_ref[...])
    border = dot_nt(high, col_ref[...]) + dot_nt(low, col_ref[...])
    early_ref[:, 5 * cap_rows, :] = border_rows(border[:tiles], border[tiles:], n_rg)


def request_kernel(n_rg, grid, width, table_rows, list_ref, got_ref, early_ref, out_ref):
    lats, lons = grid
    tiles, slots = list_ref.shape
    packed = LANES // width
    groups = lats // packed
    nlon = lons * n_rg
    for t in range(tiles):
        for f in range(slots):
            g = jnp.maximum(list_ref[t, f], 0)
            lat, lon = g // nlon, g % nlon
            key = lat // lats * n_rg + lon // lons
            inner, side = lat % lats, lon % lons
            piece = inner // groups
            row = got_ref[key, pl.ds(inner % groups * lons + side, 1), :]
            aligned = row
            for p in range(1, packed):
                aligned = jnp.where(piece == p, roll(row, -p * width, 1), aligned)
            for n, dest in ((0, t + n_rg), (1, t), (2, t - n_rg)):
                if 0 <= dest < tiles:
                    place, line = divmod(n * slots + f, table_rows)
                    put = roll(aligned, place * width, 1)
                    cut = slice(place * width, (place + 1) * width)
                    out_ref[dest, line : line + 1, cut] = put[:, cut]
        out_ref[t, table_rows:, :] = early_ref[t]


def sincos(x):
    n = jnp.floor(x * (2.0 / math.pi) + 0.5)
    r = x - n * 1.5703125
    r = r - n * 4.837512969970703e-4
    r = r - n * 7.549789954891882e-8
    z = r * r
    s = ((-1.9515295891e-4 * z + 8.3321608736e-3) * z - 1.6666654611e-1) * z * r + r
    c = ((2.443315711809948e-5 * z - 1.388731625493765e-3) * z + 4.166664568298827e-2) * z * z - 0.5 * z + 1.0
    q = n.astype(I32)
    odd = (q & 1) == 1
    sine = jnp.where(odd, c, s)
    cosine = jnp.where(odd, s, c)
    sine = jnp.where((q & 2) == 2, -sine, sine)
    cosine = jnp.where(((q + 1) & 2) == 2, -cosine, cosine)
    return cosine, sine


def flatten_kernel(width, table_rows, slots, par_ref, got_ref, image_ref, factor_ref, position_ref, one_ref, two_ref, flat_ref, edge_ref, tab_ref, in_ref, at_ref):
    even = par_ref[0] == 0
    lines, samples = factor_ref.shape
    packed = LANES // width
    tiles = got_ref.shape[0]
    parts = tiles // packed
    lane = lane_iota((table_rows, LANES))
    for k in range(parts):
        for place in range(packed):
            total = None
            for j in range(packed):
                x = roll(got_ref[k * packed + j, 0:table_rows, :], (j - place) * width, 1)
                total = x if total is None else jnp.where(lane // width == j, x, total)
            tab_ref[k, place] = total
    for i in range(3):
        top = jnp.where(even, two_ref[i], one_ref[i])
        low = jnp.where(even, one_ref[i], two_ref[i])
        in_ref[i, 0:RIM] = top
        in_ref[i, RIM + lines :] = low
    in_ref[0, RIM : RIM + lines] = image_ref[0]
    in_ref[1, RIM : RIM + lines] = image_ref[1]
    in_ref[2, RIM : RIM + lines] = factor_ref[...]
    at_ref[0:RIM] = jnp.where(even, two_ref[3], one_ref[3]).astype(I32)
    at_ref[RIM : RIM + lines] = position_ref[...]
    at_ref[RIM + lines :] = jnp.where(even, one_ref[3], two_ref[3]).astype(I32)
    cols = samples // LANES
    chunk = 16

    def block(table, start):
        at = at_ref[pl.ds(start, chunk), :]
        lanes = [at[:, j * LANES : (j + 1) * LANES] & (LANES - 1) for j in range(cols)]
        lines_at = [at[:, j * LANES : (j + 1) * LANES] // LANES for j in range(cols)]
        height = [jnp.zeros((chunk, LANES), F32) for _ in range(cols)]
        for f in range(slots):
            place, line = divmod(table * slots + f, table_rows)
            for k in range(parts):
                row = jnp.broadcast_to(tab_ref[k, place, line : line + 1, :], (chunk, LANES))
                for j in range(cols):
                    found = jnp.take_along_axis(row, lanes[j], axis=1)
                    height[j] = jnp.where(lines_at[j] == f * parts + k, found, height[j])
        for j in range(cols):
            cut = slice(j * LANES, (j + 1) * LANES)
            cosine, sine = sincos(in_ref[2, pl.ds(start, chunk), cut] * height[j])
            a, b = in_ref[0, pl.ds(start, chunk), cut], in_ref[1, pl.ds(start, chunk), cut]
            flat_ref[0, pl.ds(start, chunk), cut] = a * cosine + b * sine
            flat_ref[1, pl.ds(start, chunk), cut] = b * cosine - a * sine

    block(0, 0)

    @pl.loop(0, lines // chunk)
    def _(i):
        block(1, pl.multiple_of(RIM + i * chunk, chunk))

    block(2, RIM + lines)
    edge = lane_iota((lines + 2 * RIM, LANES))
    for c in range(2):
        first = flat_ref[c, :, 0:LANES]
        last = roll(flat_ref[c, :, samples - LANES : samples], 2 * RIM, 1)
        edge_ref[c] = jnp.where(edge < RIM, first, jnp.where(edge < 2 * RIM, last, 0.0))


def filter_kernel(n_rg, cap_rows, block_rows, rg_ref, flat_ref, edge_ref, az_h, az_l, rg_h, rg_l, back_ref, last_h, last_l, im_ref, in_ref, mask_ref, col_ref, out_ref, x_ref, d_ref, z_ref, look_ref):
    _, rows, samples = flat_ref.shape
    cols = samples // LANES
    lane = lane_iota((rows, LANES))
    left = rg_ref[0] > 0
    right = rg_ref[0] < n_rg - 1
    for c in range(2):
        halo = edge_ref[c]
        before = jnp.where(left, roll(halo, -RIM, 1), 0.0)
        after = jnp.where(right, roll(halo, RIM, 1), 0.0)
        for j in range(cols):
            now = roll(flat_ref[c, :, j * LANES : (j + 1) * LANES], RIM, 1)
            x_ref[c * rows : (c + 1) * rows, j * LANES : (j + 1) * LANES] = jnp.where(lane < RIM, before, now)
            before = now
        x_ref[c * rows : (c + 1) * rows, cols * LANES :] = jnp.where(
            lane < RIM, before, jnp.where(lane < 2 * RIM, after, 0.0)
        )
    high, low = split(x_ref[...])
    g = dot(az_h[...], high) + dot(az_h[...], low) + dot(az_l[...], high)
    count = block_rows * PATCH
    pieces = LANES // HALF
    for j in range(cols + 1):
        cut = slice(j * LANES, (j + 1) * LANES)
        both = jnp.concatenate([g[:count, cut], g[count:, cut]], axis=1)
        bh, bl = split(both)
        used = pieces if j < cols else 1
        wide = slice(0, used * 2 * PATCH)
        d = dot(bh, rg_h[:, wide]) + dot(bl, rg_h[:, wide]) + dot(bh, rg_l[:, wide])
        for q in range(used):
            d_ref[j * pieces + q] = d[:, q * 2 * PATCH : (q + 1) * 2 * PATCH]
    sign = jnp.where(lane_iota((1, LANES)) % 2 == 0, 1.0, -1.0)
    patches = samples // STEP

    @pl.loop(0, patches)
    def _(v):
        z = d_ref[v] + sign * d_ref[v + 1]
        q = z * z
        q = q + pltpu.roll(q, PATCH, 1)
        magnitude = jnp.sqrt(q)
        s = magnitude + pltpu.roll(magnitude, 1, 1) + pltpu.roll(magnitude, LANES - 1, 1)
        parts = []
        for u in range(block_rows):
            cut = slice(u * PATCH, (u + 1) * PATCH)
            su = s[cut]
            su = su + pltpu.roll(su, 1, 0) + pltpu.roll(su, PATCH - 1, 0)
            mean = jnp.sum(magnitude[cut], keepdims=True) * (1.0 / (2 * PATCH * PATCH))
            factor = 1.0 / (9.0 * (mean + EPS))
            parts.append(z[cut] * jnp.sqrt(su * factor))
        high, low = split(jnp.concatenate(parts, axis=0))
        at = pl.multiple_of(v * LANES, LANES)
        z_ref[0:count, pl.ds(at, LANES)] = high
        z_ref[count:, pl.ds(at, LANES)] = low

    t = dot(back_ref[...], z_ref[...])
    looks = block_rows * STEP // LOOK
    t = t[: 2 * looks] + t[2 * looks :]
    stacked = jnp.concatenate(
        [
            jnp.concatenate([t[:looks, v * LANES : (v + 1) * LANES], t[looks:, v * LANES : (v + 1) * LANES]], axis=1)
            for v in range(patches)
        ],
        axis=0,
    )
    sh, sl = split(stacked)
    y = dot(sh, last_h[...]) + dot(sl, last_h[...]) + dot(sh, last_l[...])
    group = lane_iota((looks, LANES)) // (STEP // LOOK)
    for c in range(2):
        total = jnp.zeros((looks, LANES), F32)
        for v in range(patches):
            part = y[v * looks : (v + 1) * looks, c * LANES : (c + 1) * LANES]
            total = jnp.where(group == v, part, total)
        look_ref[c] = total
    tiles = out_ref.shape[0]
    for k in range(cap_rows):
        cut = slice(k * LANES, (k + 1) * LANES)
        at_m, at_n = im_ref[:, cut], in_ref[:, cut]
        for c in range(2):
            total = jnp.zeros((tiles, LANES), F32)
            for m in range(looks):
                total = jnp.where(at_m == m, lane_gather(look_ref[c, m : m + 1, :], at_n), total)
            out_ref[:, c * cap_rows + k, :] = total
    for c in range(2):
        weighted = jnp.concatenate(
            [mask_ref[:, m * LANES : (m + 1) * LANES] * look_ref[c, m : m + 1, :] for m in range(looks)], axis=1
        )
        wh, wl = split(weighted)
        border = dot_nt(wh, col_ref[...]) + dot_nt(wl, col_ref[...])
        out_ref[:, 2 * cap_rows + c, :] = border_rows(border[:tiles], border[tiles:], n_rg)


def prepare_kernel(cap_rows, table_rows, map_lat, got_ref, hot_ref, row_ref, sum_ref, carry_ref):
    tiles = got_ref.shape[0]
    for t in range(tiles):
        for k in range(cap_rows):
            def channel(c):
                return got_ref[t, table_rows + c * cap_rows + k : table_rows + c * cap_rows + k + 1, :]

            cell = channel(4).astype(I32)
            line, column = cell // LANES, cell % LANES
            at = (t * cap_rows + k) * LANES
            cut = slice(at, at + LANES)
            hot_ref[:, cut] = (row_iota((LANES, LANES)) == column).astype(F32).astype(BF16)
            rows = row_iota((map_lat, LANES))
            here, next_line = rows == line, rows == line + 1
            for d in range(2):
                row_ref[d * map_lat : (d + 1) * map_lat, cut] = jnp.where(here, channel(d), 0.0) + jnp.where(
                    next_line, channel(2 + d), 0.0
                )
    high, low = split(row_ref[...])
    acc = dot_nt(high, hot_ref[...]) + dot_nt(low, hot_ref[...])
    shifted = roll(acc[map_lat:], 1, 1)
    lane = lane_iota(shifted.shape)
    edge = got_ref[0, table_rows + 5 * cap_rows : table_rows + 5 * cap_rows + 1, :]
    for t in range(1, tiles):
        edge = edge + got_ref[t, table_rows + 5 * cap_rows : table_rows + 5 * cap_rows + 1, :]
    total = acc[:map_lat] + jnp.where(lane == 0, 0.0, shifted)
    sum_ref[...] = total + jnp.where(row_iota(shifted.shape) == 0, edge, 0.0)
    carry_ref[...] = jnp.where(lane == 0, shifted, 0.0)


def splat_kernel(cap_rows, map_lat, got_ref, hot_ref, row_ref, sum_ref, carry_ref, x_ref):
    tiles = got_ref.shape[0]
    wide = 2 * map_lat
    for t in range(tiles):
        for k in range(cap_rows):
            cut = slice((t * cap_rows + k) * LANES, (t * cap_rows + k + 1) * LANES)
            for c in range(2):
                value = got_ref[t, c * cap_rows + k : c * cap_rows + k + 1, :]
                high, low = split(row_ref[:, cut] * value)
                x_ref[c * wide : (c + 1) * wide, cut] = high
                x_ref[(2 + c) * wide : (3 + c) * wide, cut] = low
    acc = dot_nt(x_ref[...], hot_ref[...])
    acc = acc[: 2 * wide] + acc[2 * wide :]
    for c in range(2):
        row = 2 * cap_rows + c
        edge = got_ref[0, row : row + 1, :]
        for t in range(1, tiles):
            edge = edge + got_ref[t, row : row + 1, :]
        shifted = roll(acc[c * wide + map_lat : (c + 1) * wide], 1, 1)
        lane = lane_iota(shifted.shape)
        total = acc[c * wide : c * wide + map_lat] + jnp.where(lane == 0, 0.0, shifted)
        sum_ref[c] = total + jnp.where(row_iota(shifted.shape) == 0, edge, 0.0)
        carry_ref[c] = jnp.where(lane == 0, shifted, 0.0)


def swap_pairs(count, first):
    return [p for i in range(first, count - 1, 2) for p in ((i, i + 1), (i + 1, i))]


def body(image, factor, heights, listing, position, owner, base, shares):
    n_az, n_rg = lax.axis_size("az"), lax.axis_size("rg")
    tiles = n_az * n_rg
    both = ("az", "rg")
    lats, lons, points = heights.shape
    slots = listing.shape[1]
    width = points // tiles
    packed = LANES // width
    lines, samples = factor.shape
    map_lat, map_lon = lines // LOOK, samples // LOOK
    block_rows = lines // STEP
    capacity = 2 * map_lat * map_lon // tiles
    cap_rows = -(-capacity // LANES)
    table_rows = -(-3 * slots // packed)
    table_rows = -(-table_rows // 8) * 8
    early_rows = -(-(5 * cap_rows + 1) // 8) * 8
    late_rows = -(-(2 * cap_rows + 2) // 8) * 8
    slice_rows = lats * lons // packed
    parity = (lax.axis_index("az") % 2).astype(I32).reshape(1)
    rg = lax.axis_index("rg").astype(I32).reshape(1)

    def exchange(x):
        return lax.all_to_all(x, both, split_axis=0, concat_axis=0, tiled=True)

    slices = call(
        functools.partial(slice_kernel, width),
        sds((tiles, slice_rows + 8, LANES)),
        (heights, listing),
    )
    got_slices = exchange(slices)
    one, two = call(halo_kernel, [sds((4, RIM, samples))] * 2, (parity, image, factor, position), smem=(0,))
    one = lax.ppermute(one, "az", swap_pairs(n_az, 0))
    two = lax.ppermute(two, "az", swap_pairs(n_az, 1))
    total = map_lat * map_lon
    early, at_m, at_n, edge_mask, edge_col = call(
        functools.partial(pack_kernel, n_rg, cap_rows),
        [
            sds((tiles, early_rows, LANES)),
            sds((tiles, cap_rows * LANES), I32),
            sds((tiles, cap_rows * LANES), I32),
            sds((2 * tiles, total)),
            sds((map_lon, total), BF16),
        ],
        (owner.reshape(map_lat, map_lon), base.reshape(map_lat, map_lon), shares.reshape(4, map_lat, map_lon)),
        scratch=(VMEM((cap_rows * LANES, total), BF16), VMEM((3 * tiles, total), BF16)),
    )
    lists = got_slices[:, slice_rows, :slots].astype(I32)
    request = call(
        functools.partial(request_kernel, n_rg, (lats, lons), width, table_rows),
        sds((tiles, table_rows + early_rows, LANES)),
        (lists, got_slices, early),
        smem=(0,),
    )
    tables = exchange(request)
    flat, edge = call(
        functools.partial(flatten_kernel, width, table_rows, slots),
        [sds((2, lines + 2 * RIM, samples)), sds((2, lines + 2 * RIM, LANES))],
        (parity, tables, image, factor, position, one, two),
        smem=(0,),
        scratch=(
            VMEM((tiles // packed, packed, table_rows, LANES), F32),
            VMEM((3, lines + 2 * RIM, samples), F32),
            VMEM((lines + 2 * RIM, samples), I32),
        ),
    )
    edge = lax.ppermute(edge, "rg", swap_pairs(n_rg, 0))
    az, rgt, back, last = filter_tables(block_rows)
    az_h, az_l = host_split(az)
    rg_h, rg_l = host_split(rgt)
    back_h, back_l = host_split(back)
    back_all = np.concatenate(
        [np.concatenate([back_h, back_h], axis=1), np.concatenate([back_l, np.zeros_like(back_l)], axis=1)], axis=0
    )
    last_h, last_l = host_split(last)
    rows = lines + 2 * RIM
    patches = samples // STEP
    count = block_rows * PATCH
    packed_looks = call(
        functools.partial(filter_kernel, n_rg, cap_rows, block_rows),
        sds((tiles, late_rows, LANES)),
        (rg, flat, edge, az_h, az_l, rg_h, rg_l, back_all, last_h, last_l, at_m, at_n, edge_mask, edge_col),
        smem=(0,),
        scratch=(
            VMEM((2 * rows, samples + LANES), F32),
            VMEM((patches + 1 + 3, count, 2 * PATCH), F32),
            VMEM((2 * count, patches * LANES), BF16),
            VMEM((2, map_lat, map_lon), F32),
        ),
    )
    got = exchange(packed_looks)
    wide = tiles * cap_rows * LANES
    hot, row_weights, weight_sum, weight_carry = call(
        functools.partial(prepare_kernel, cap_rows, table_rows, map_lat),
        [sds((LANES, wide), BF16), sds((2 * map_lat, wide)), sds((map_lat, map_lon)), sds((map_lat, map_lon))],
        (tables,),
    )
    right = [(i, i + 1) for i in range(n_rg - 1)]
    weight_sum = weight_sum + lax.ppermute(weight_carry, "rg", right)
    sums, carry = call(
        functools.partial(splat_kernel, cap_rows, map_lat),
        [sds((2, map_lat, map_lon)), sds((2, map_lat, map_lon))],
        (got, hot, row_weights),
        scratch=(VMEM((8 * map_lat, wide), BF16),),
    )
    sums = sums + lax.ppermute(carry, "rg", right)
    return sums / jnp.maximum(weight_sum, 1.0)[None]


def solution(mesh):
    return jax.shard_map(
        body,
        mesh=mesh,
        in_specs=(
            P(None, ("scene", "az"), "rg"),
            P(("scene", "az"), "rg"),
            P(("scene", "az"), "rg", None),
            P(("scene", "az", "rg"), None),
            P(("scene", "az"), "rg"),
            P(("scene", "az", "rg"), None),
            P(("scene", "az", "rg")),
            P(None, ("scene", "az", "rg")),
        ),
        out_specs=P(None, ("scene", "az"), "rg"),
        check_vma=False,
    )
```

```python
import functools
import math

import jax
import jax.numpy as jnp
import numpy as np
from jax import lax
from jax.experimental import pallas as pl
from jax.experimental.pallas import tpu as pltpu
from jax.sharding import PartitionSpec as P

PATCH = 64
LOOK = 4
EPS = 1e-06
LANES = 128
RIM = PATCH // 4
STEP = PATCH // 2
HALF = PATCH // 2
F32 = jnp.float32
BF16 = jnp.bfloat16
I32 = jnp.int32
VMEM = pltpu.VMEM
VSPEC = pl.BlockSpec(memory_space=pltpu.VMEM)
SSPEC = pl.BlockSpec(memory_space=pltpu.SMEM)


def call(kernel, outs, args, scratch=(), smem=(), grant=16, cost=(1_000_000, 1_000_000)):
    return pl.pallas_call(
        kernel,
        out_shape=outs,
        in_specs=[SSPEC if i in smem else VSPEC for i in range(len(args))],
        out_specs=jax.tree.map(lambda _: VSPEC, outs),
        scratch_shapes=list(scratch),
        compiler_params=pltpu.CompilerParams(vmem_limit_bytes=grant << 20),
        cost_estimate=pl.CostEstimate(flops=cost[0], bytes_accessed=cost[1], transcendentals=0),
    )(*args)


def sds(shape, dtype=F32):
    return jax.ShapeDtypeStruct(shape, dtype)


def split(x):
    hi = x.astype(BF16)
    return hi, (x - hi.astype(F32)).astype(BF16)


def dot(a, b):
    return jnp.dot(a, b, preferred_element_type=F32)


def dot_nt(a, b):
    return lax.dot_general(a, b, (((1,), (1,)), ((), ())), preferred_element_type=F32)


def fetch(pairs, sems):
    copies = [pltpu.make_async_copy(src, dst, sems.at[i]) for i, (src, dst) in enumerate(pairs)]
    for copy in copies:
        copy.start()
    return copies


def lane_iota(shape):
    return lax.broadcasted_iota(I32, shape, len(shape) - 1)


def row_iota(shape):
    return lax.broadcasted_iota(I32, shape, 0)


def roll(x, shift, axis):
    shift = shift % x.shape[axis]
    return x if shift == 0 else pltpu.roll(x, shift, axis)


def lane_gather(row, index):
    return jnp.take_along_axis(jnp.broadcast_to(row, index.shape), index, axis=1)


def host_split(x):
    hi = np.asarray(x, np.float32).astype(BF16)
    lo = (np.asarray(x, np.float64) - hi.astype(np.float64)).astype(BF16)
    return hi, lo


UNROLL = 2


def filter_tables(block_rows):
    turn = 2.0 * math.pi / PATCH
    step = np.arange(PATCH)
    cosine = np.cos(turn * (step[:, None] * step[None, :] % PATCH))
    sine = np.sin(turn * (step[:, None] * step[None, :] % PATCH))
    count = block_rows * PATCH
    az = np.zeros((2 * PATCH, 2 * HALF))
    az[:PATCH, :HALF], az[:PATCH, HALF:] = cosine[:, :HALF], sine[:, :HALF]
    az[PATCH:, :HALF], az[PATCH:, HALF:] = -sine[:, :HALF], cosine[:, :HALF]
    pieces = LANES // HALF
    rg = np.zeros((2 * LANES, pieces * 2 * PATCH))
    for q in range(pieces):
        w = slice(q * HALF, (q + 1) * HALF)
        wi = slice(LANES + q * HALF, LANES + (q + 1) * HALF)
        lr = slice(q * 2 * PATCH, q * 2 * PATCH + PATCH)
        li = slice(q * 2 * PATCH + PATCH, (q + 1) * 2 * PATCH)
        rg[w, lr], rg[wi, lr] = cosine[:HALF], sine[:HALF]
        rg[w, li], rg[wi, li] = -sine[:HALF], cosine[:HALF]
    looks = STEP // LOOK
    core = cosine[RIM : RIM + STEP].reshape(looks, LOOK, PATCH).mean(axis=1)
    core_s = sine[RIM : RIM + STEP].reshape(looks, LOOK, PATCH).mean(axis=1)
    back = np.zeros((2 * block_rows * looks, count))
    for u in range(block_rows):
        k = slice(u * PATCH, (u + 1) * PATCH)
        back[u * looks : (u + 1) * looks, k] = core / PATCH
        back[(block_rows + u) * looks : (block_rows + u + 1) * looks, k] = core_s / PATCH
    c_l, s_l = core.T / PATCH, core_s.T / PATCH
    reps = LANES // looks
    last = np.concatenate(
        [
            np.concatenate([np.tile(c_l, reps), np.tile(s_l, reps)], axis=1),
            np.concatenate([np.tile(-s_l, reps), np.tile(c_l, reps)], axis=1),
            np.concatenate([np.tile(-s_l, reps), np.tile(c_l, reps)], axis=1),
            np.concatenate([np.tile(-c_l, reps), np.tile(-s_l, reps)], axis=1),
        ],
        axis=0,
    )
    return az, rg, back, last


def slice_kernel(width, dem_ref, list_ref, out_ref):
    tiles = out_ref.shape[0]
    lats, lons, _ = dem_ref.shape
    packed = LANES // width
    groups = lats // packed
    slots = list_ref.shape[1]
    lane = lane_iota((lons, LANES))
    listed = list_ref[...].astype(F32)
    for q in range(tiles):
        tile, offset = divmod(q * width, LANES)
        for g in range(groups):
            total = None
            for p in range(packed):
                x = dem_ref[p * groups + g, :, tile * LANES : (tile + 1) * LANES]
                x = roll(x, p * width - offset, 1)
                total = x if total is None else jnp.where(lane // width == p, x, total)
            out_ref[q, g * lons : (g + 1) * lons, :] = total
        out_ref[q, groups * lons : groups * lons + 1, 0:slots] = listed


def halo_kernel(par_ref, image_ref, factor_ref, position_ref, one_ref, two_ref):
    even = par_ref[0] == 0
    lines = factor_ref.shape[0]
    fields = (
        lambda s: image_ref[0, s, :],
        lambda s: image_ref[1, s, :],
        lambda s: factor_ref[s, :],
        lambda s: position_ref[s, :].astype(F32),
    )
    for i, field in enumerate(fields):
        first = field(slice(0, RIM))
        last = field(slice(lines - RIM, lines))
        one_ref[i] = jnp.where(even, last, first)
        two_ref[i] = jnp.where(even, first, last)


def border_sums(n_rg, tiles, values, owner_ref, base_ref, share_ref, w_ref, col_ref, here_ref, next_ref):
    channels = len(values)
    height, width = owner_ref.shape
    base = base_ref[...]
    last_line = jnp.right_shift(base, width.bit_length() - 1) == height - 1
    last_column = jnp.bitwise_and(base, width - 1) == width - 1
    owner = owner_ref[...]
    on_line = jnp.where(last_line, owner, -1)
    on_column = jnp.where(last_column, owner, -1)
    terms = []
    for c, value in enumerate(values):
        for i in range(2):
            spot = (i * channels + c) * tiles
            far = 4 * channels * tiles + spot
            for mask, k, row in ((0, 2, 2 * spot), (0, 3, 2 * spot + tiles), (1, 1, far), (1, 3, far + 2 * channels * tiles)):
                x = share_ref[k] if value is None else share_ref[k] * value
                high = x.astype(BF16).astype(F32)
                terms.append((mask, row, high if i == 0 else x - high))
    tile = row_iota((tiles, width))
    for m in range(height):
        cut = slice(m * width, (m + 1) * width)
        masks = (tile == on_line[m : m + 1], tile == on_column[m : m + 1])
        for mask, row, x in terms:
            w_ref[row : row + tiles, cut] = jnp.where(masks[mask], x[m : m + 1], 0.0).astype(BF16)
    size = channels * tiles
    b = dot_nt(w_ref[0 : 4 * size], col_ref[...])
    b = b[: 2 * size] + b[2 * size :]
    side = dot_nt(w_ref[4 * size : 6 * size], here_ref[...]) + dot_nt(w_ref[6 * size : 8 * size], next_ref[...])
    side = side[:size] + side[size:]
    results = []
    for c in range(channels):
        b0, b1 = b[2 * c * tiles : (2 * c + 1) * tiles], b[(2 * c + 1) * tiles : (2 * c + 2) * tiles]
        dest = row_iota(b0.shape)
        shifted = roll(b1, 1, 1)
        below = roll(b0, n_rg, 0)
        beside = roll(shifted, n_rg, 0)
        diagonal = jnp.where(dest % n_rg > 0, roll(shifted, n_rg + 1, 0), 0.0)
        beside = jnp.where(lane_iota(b0.shape) == 0, diagonal, beside)
        rows = jnp.where(dest >= n_rg, below + beside, 0.0)
        one = side[c * tiles : (c + 1) * tiles]
        one = jnp.concatenate([jnp.zeros((1, one.shape[1]), F32), one[:-1]], axis=0)
        results.append((rows, jnp.where(row_iota(one.shape) % n_rg > 0, one, 0.0)))
    return results


def add_edges(total, edges, channel, first):
    rows, lanes = row_iota(total.shape), lane_iota(total.shape)
    edge, side = edges[first + channel : first + channel + 1], edges[first + 3 : first + 4]
    column = jnp.sum(jnp.where(lanes == rows + channel * total.shape[0], side, 0.0), axis=1, keepdims=True)
    return total + jnp.where(rows == 0, edge, 0.0) + jnp.where(lanes == 0, column, 0.0)


def pack_kernel(n_rg, cap_rows, owner_ref, base_ref, share_ref, early_ref, cell_ref, rim_ref, side_ref, im_ref, in_ref, col_ref, here_ref, next_ref, hot_ref, lhs_ref, w_ref):
    tiles = early_ref.shape[0]
    height, width = owner_ref.shape
    owner = owner_ref[...]
    batch = min(tiles, 16)
    tri = (row_iota((width, width)) < lane_iota((width, width))).astype(BF16)
    ones = jnp.ones((width, width), BF16)
    size = batch * height
    r, c = row_iota((size, size)), lane_iota((size, size))
    lower = ((r // height == c // height) & (c < r)).astype(BF16)
    rank = jnp.zeros((height, width), F32)
    for b in range(tiles // batch):
        hot = jnp.concatenate([(owner == b * batch + o).astype(F32) for o in range(batch)], axis=0)
        hot16 = hot.astype(BF16)
        before = dot(hot16, tri) + dot(lower, dot(hot16, ones).astype(BF16))
        kept = hot * before
        for o in range(batch):
            rank = rank + kept[o * height : (o + 1) * height]
    rank = rank.astype(I32)
    base = base_ref[...]
    shift = width.bit_length() - 1
    column = jnp.bitwise_and(base, width - 1)
    line = jnp.right_shift(base, shift)
    cap = cap_rows * LANES
    for m in range(height):
        cut = slice(m * width, (m + 1) * width)
        hot_ref[:, cut] = (row_iota((cap, width)) == rank[m : m + 1]).astype(F32).astype(BF16)
        col_ref[:, cut] = (row_iota((width, width)) == column[m : m + 1]).astype(F32).astype(BF16)
        mine = row_iota((tiles, width)) == owner[m : m + 1]
        lhs_ref[0:tiles, cut] = mine.astype(F32).astype(BF16)
        lhs_ref[tiles : 2 * tiles, cut] = jnp.where(mine, float(m), 0.0).astype(BF16)
        lhs_ref[2 * tiles :, cut] = jnp.where(mine, lane_iota((tiles, width)).astype(F32), 0.0).astype(BF16)
        at = row_iota((height, width))
        here_ref[:, cut] = (at == line[m : m + 1]).astype(F32).astype(BF16)
        next_ref[:, cut] = (at == line[m : m + 1] + 1).astype(F32).astype(BF16)
    found = dot_nt(lhs_ref[...], hot_ref[...])
    valid = found[0:tiles] > 0.5
    at_m = found[tiles : 2 * tiles].astype(I32)
    at_n = found[2 * tiles :].astype(I32)
    im_ref[...] = at_m
    in_ref[...] = at_n
    cell = base.astype(F32)
    for channel in range(5):
        for k in range(cap_rows):
            cut = slice(k * LANES, (k + 1) * LANES)
            total = jnp.zeros((tiles, LANES), F32)
            for m in range(height):
                row = cell[m : m + 1] if channel == 4 else share_ref[channel, m : m + 1, :]
                total = jnp.where(at_m[:, cut] == m, lane_gather(row, at_n[:, cut]), total)
            total = jnp.where(valid[:, cut], total, 0.0)
            if channel == 4:
                cell_ref[:, cut] = total
            else:
                early_ref[:, channel * cap_rows + k, :] = total
    ((rows, side),) = border_sums(n_rg, tiles, [None], owner_ref, base_ref, share_ref, w_ref, col_ref, here_ref, next_ref)
    rim_ref[...] = rows
    side_ref[...] = side


def request_kernel(n_rg, grid, width, table_rows, slots, got_ref, early_ref, cell_ref, out_ref, turn_ref, list_ref, index_ref, sem):
    tiles, rows, _ = got_ref.shape
    lats, lons = grid
    packed = LANES // width
    groups = lats // packed
    listed = jnp.maximum(got_ref[:, rows - 8, :], 0.0)
    listed = jnp.where(lane_iota(listed.shape) < slots, listed, 0.0).astype(I32)
    lat, lon = listed // (lons * n_rg), listed % (lons * n_rg)
    key = lat // lats * n_rg + lon // lons
    list_ref[0] = key * rows + lat % lats % groups * lons + lon % lons
    list_ref[1] = lat % lats // groups
    (copy,) = fetch(((list_ref, index_ref),), sem)
    for t in range(tiles):
        x = got_ref[t]
        for p in range(packed):
            turn_ref[p, t * rows : (t + 1) * rows, :] = roll(x, p * width, 1)
        out_ref[t, table_rows:, :] = early_ref[t]
    for k in range(cell_ref.shape[1] // LANES):
        x = cell_ref[:, k * LANES : (k + 1) * LANES]
        for i in range(packed):
            place, line = divmod(3 * slots + k * packed + i, table_rows)
            cut = slice(place * width, (place + 1) * width)
            out_ref[:, line, cut] = roll(x, (place - i) * width, 1)[:, cut]
    copy.wait()
    for t in range(tiles):
        for f in range(slots):
            row, piece = index_ref[0, t, f], index_ref[1, t, f]
            for n, dest in ((0, t + n_rg), (1, t), (2, t - n_rg)):
                if 0 <= dest < tiles:
                    place, line = divmod(n * slots + f, table_rows)
                    turn = jnp.bitwise_and(place - piece, packed - 1)
                    put = turn_ref[turn, pl.ds(row, 1), :]
                    cut = slice(place * width, (place + 1) * width)
                    out_ref[dest, line : line + 1, cut] = put[:, cut]


def sincos(x):
    n = jnp.floor(x * (2.0 / math.pi) + 0.5)
    r = x - n * 1.5703125
    r = r - n * 4.837512969970703e-4
    r = r - n * 7.549789954891882e-8
    z = r * r
    s = ((-1.9515295891e-4 * z + 8.3321608736e-3) * z - 1.6666654611e-1) * z * r + r
    c = ((2.443315711809948e-5 * z - 1.388731625493765e-3) * z + 4.166664568298827e-2) * z * z - 0.5 * z + 1.0
    q = n.astype(I32)
    odd = (q & 1) == 1
    sine = jnp.where(odd, c, s)
    cosine = jnp.where(odd, s, c)
    sine = jnp.where((q & 2) == 2, -sine, sine)
    cosine = jnp.where(((q + 1) & 2) == 2, -cosine, cosine)
    return cosine, sine


def flatten_kernel(width, table_rows, slots, par_ref, got_ref, image_ref, factor_ref, position_ref, one_ref, two_ref, flat_ref, edge_ref, tab_ref, in_ref, at_ref):
    even = par_ref[0] == 0
    lines, samples = factor_ref.shape
    packed = LANES // width
    tiles = got_ref.shape[0]
    parts = tiles // packed
    lane = lane_iota((table_rows, LANES))
    for k in range(parts):
        for place in range(packed):
            total = None
            for j in range(packed):
                x = roll(got_ref[k * packed + j, 0:table_rows, :], (j - place) * width, 1)
                total = x if total is None else jnp.where(lane // width == j, x, total)
            tab_ref[k, place * table_rows : (place + 1) * table_rows, :] = total
    for i in range(3):
        top = jnp.where(even, two_ref[i], one_ref[i])
        low = jnp.where(even, one_ref[i], two_ref[i])
        in_ref[i, 0:RIM] = top
        in_ref[i, RIM + lines :] = low
    in_ref[0, RIM : RIM + lines] = image_ref[0]
    in_ref[1, RIM : RIM + lines] = image_ref[1]
    in_ref[2, RIM : RIM + lines] = factor_ref[...]
    at_ref[0:RIM] = jnp.where(even, two_ref[3], one_ref[3]).astype(I32)
    at_ref[RIM : RIM + lines] = position_ref[...]
    at_ref[RIM + lines :] = jnp.where(even, one_ref[3], two_ref[3]).astype(I32)
    pairs = samples // LANES // 2
    steps = (lines + 2 * RIM) // 8 * pairs
    rim_steps = RIM // 8 * pairs
    shift = LANES.bit_length() - 1

    def spots(i):
        start = pl.multiple_of(i // pairs * 8, 8)
        return [(pl.ds(start, 8), pl.ds(pl.multiple_of((i % pairs * 2 + j) * LANES, LANES), LANES)) for j in range(2)]

    def lookup(i):
        base = jnp.where(i < rim_steps, 0, jnp.where(i < steps - rim_steps, slots, 2 * slots))
        at = [at_ref[spot] for spot in spots(i)]
        lanes = [jnp.bitwise_and(x, LANES - 1) for x in at]
        lines_at = [jnp.right_shift(x, shift) for x in at]
        height = [jnp.zeros((8, LANES), F32) for _ in range(2)]
        for f in range(slots):
            for k in range(parts):
                row = jnp.broadcast_to(tab_ref[k, pl.ds(base + f, 1), :], (8, LANES))
                for j in range(2):
                    found = jnp.take_along_axis(row, lanes[j], axis=1)
                    height[j] = jnp.where(lines_at[j] == f * parts + k, found, height[j])
        return tuple(height)

    def finish(i, height):
        for spot, h in zip(spots(i), height):
            cosine, sine = sincos(in_ref[(2, *spot)] * h)
            a, b = in_ref[(0, *spot)], in_ref[(1, *spot)]
            flat_ref[(0, *spot)] = a * cosine + b * sine
            flat_ref[(1, *spot)] = b * cosine - a * sine

    def step(i, height):
        found = lookup(i)
        finish(i - 1, height)
        return found

    finish(steps - 1, lax.fori_loop(1, steps, step, lookup(0)))
    edge = lane_iota((lines + 2 * RIM, LANES))
    for c in range(2):
        first = flat_ref[c, :, 0:LANES]
        last = roll(flat_ref[c, :, samples - LANES : samples], 2 * RIM, 1)
        edge_ref[c] = jnp.where(edge < RIM, first, jnp.where(edge < 2 * RIM, last, 0.0))


def root(x):
    return x * lax.rsqrt(jnp.maximum(x, 1e-37))


def filter_kernel(n_rg, cap_rows, block_rows, rg_ref, flat_ref, edge_ref, rim_ref, side_ref, im_ref, in_ref, owner_ref, base_ref, share_ref, const_ref, col_ref, here_ref, next_ref, out_ref, x_ref, d_ref, s_ref, p_ref, z_ref, look_ref, w_ref):
    _, rows, samples = flat_ref.shape
    cols = samples // LANES
    wide = (cols + 1) * LANES
    lane = lane_iota((HALF, LANES))
    left = rg_ref[0] > 0
    right = rg_ref[0] < n_rg - 1
    strips = rows // HALF
    for p in range(strips):
        for c in range(2):
            cut = slice(p * HALF, (p + 1) * HALF)
            halo = edge_ref[c, cut]
            before = jnp.where(left, roll(halo, -RIM, 1), 0.0)
            after = jnp.where(right, roll(halo, RIM, 1), 0.0)
            for j in range(cols + 1):
                if j < cols:
                    now = roll(flat_ref[c, cut, j * LANES : (j + 1) * LANES], RIM, 1)
                else:
                    now = jnp.where(lane < 2 * RIM, after, 0.0)
                high, low = split(jnp.where(lane < RIM, before, now))
                before = now
                at = slice(p * wide + j * LANES, p * wide + (j + 1) * LANES)
                x_ref[c * HALF : (c + 1) * HALF, at] = high
                x_ref[(2 + c) * HALF : (3 + c) * HALF, at] = low
                x_ref[(4 + c) * HALF : (5 + c) * HALF, at] = high
    looks = block_rows * STEP // LOOK
    tall = [slice(i * 2 * LANES, (i + 1) * 2 * LANES) for i in range(3)]
    rg_h, rg_l = const_ref[tall[0]], const_ref[tall[1]]
    last_h, last_l = const_ref[tall[2], : 2 * LANES], const_ref[tall[2], 2 * LANES :]
    az = const_ref[6 * LANES : 6 * LANES + 2 * PATCH, : 6 * HALF]
    back = const_ref[6 * LANES : 6 * LANES + 4 * looks, 2 * LANES :]
    e = dot(az, x_ref[...])
    count = block_rows * PATCH
    pieces = LANES // HALF
    flip = jnp.where(row_iota((PATCH, LANES)) % 2 == 0, 1.0, -1.0)

    def spectrum(c, j):
        cells = []
        for u in range(block_rows):
            one = e[c * PATCH : (c + 1) * PATCH, u * wide + j * LANES : u * wide + (j + 1) * LANES]
            two = e[c * PATCH : (c + 1) * PATCH, (u + 1) * wide + j * LANES : (u + 1) * wide + (j + 1) * LANES]
            cells.append(one + flip * two)
        return jnp.concatenate(cells, axis=0)

    both = jnp.concatenate(
        [jnp.concatenate([spectrum(0, j), spectrum(1, j)], axis=1) for j in range(cols + 1)], axis=0
    )
    bh, bl = split(both)
    for start, stop, used in ((0, cols, pieces), (cols, cols + 1, 1)):
        span = slice(0, used * 2 * PATCH)
        tall = slice(start * count, stop * count)
        d = dot(bh[tall], rg_h[:, span]) + dot(bl[tall], rg_h[:, span]) + dot(bh[tall], rg_l[:, span])
        for j in range(start, stop):
            for q in range(used):
                d_ref[j * pieces + q] = d[(j - start) * count : (j - start + 1) * count, q * 2 * PATCH : (q + 1) * 2 * PATCH]
    sign = jnp.where(lane_iota((1, LANES)) % 2 == 0, 1.0, -1.0)
    patches = samples // STEP

    @pl.loop(0, patches, unroll=UNROLL)
    def _(v):
        z = d_ref[v] + sign * d_ref[v + 1]
        d_ref[v] = z
        q = z * z
        magnitude = root(q + pltpu.roll(q, PATCH, 1))
        s = magnitude + pltpu.roll(magnitude, 1, 1) + pltpu.roll(magnitude, LANES - 1, 1)
        for u in range(block_rows):
            cut = slice(u * PATCH, (u + 1) * PATCH)
            su = s[cut]
            s_ref[v, cut] = su + pltpu.roll(su, 1, 0) + pltpu.roll(su, PATCH - 1, 0)
            part = magnitude[u * PATCH : u * PATCH + 8]
            for i in range(1, PATCH // 8):
                part = part + magnitude[u * PATCH + 8 * i : u * PATCH + 8 * i + 8]
            p_ref[v, u] = part

    for v in range(patches):
        mean = jnp.sum(p_ref[v], axis=(1, 2), keepdims=True) * (1.0 / (2 * PATCH * PATCH))
        p_ref[v] = jnp.broadcast_to(1.0 / (9.0 * (mean + EPS)), p_ref.shape[1:])

    @pl.loop(0, patches, unroll=UNROLL)
    def _(v):
        at = pl.multiple_of(v * LANES, LANES)
        for u in range(block_rows):
            cut = slice(u * PATCH, (u + 1) * PATCH)
            factor = jnp.concatenate([p_ref[v, u]] * (PATCH // 8), axis=0)
            high, low = split(d_ref[v, cut] * root(s_ref[v, cut] * factor))
            z_ref[cut, pl.ds(at, LANES)] = high
            z_ref[count + u * PATCH : count + (u + 1) * PATCH, pl.ds(at, LANES)] = low

    t = dot(back, z_ref[...])
    t = t[: 2 * looks] + t[2 * looks :]
    stacked = jnp.concatenate(
        [
            jnp.concatenate([t[:looks, v * LANES : (v + 1) * LANES], t[looks:, v * LANES : (v + 1) * LANES]], axis=1)
            for v in range(patches)
        ],
        axis=0,
    )
    sh, sl = split(stacked)
    y = dot(sh, last_h) + dot(sl, last_h) + dot(sh, last_l)
    group = lane_iota((looks, LANES)) // (STEP // LOOK)
    for c in range(2):
        total = jnp.zeros((looks, LANES), F32)
        for v in range(patches):
            part = y[v * looks : (v + 1) * looks, c * LANES : (c + 1) * LANES]
            total = jnp.where(group == v, part, total)
        look_ref[c] = total
    tiles = out_ref.shape[0]
    for k in range(cap_rows):
        cut = slice(k * LANES, (k + 1) * LANES)
        at_m, at_n = im_ref[:, cut], in_ref[:, cut]
        for c in range(2):
            total = jnp.zeros((tiles, LANES), F32)
            for m in range(looks):
                total = jnp.where(at_m == m, lane_gather(look_ref[c, m : m + 1, :], at_n), total)
            out_ref[:, c * cap_rows + k, :] = total
    values = [look_ref[0], look_ref[1]]
    borders = border_sums(n_rg, tiles, values, owner_ref, base_ref, share_ref, w_ref, col_ref, here_ref, next_ref)
    for c, (rows, side) in enumerate(borders):
        out_ref[:, 2 * cap_rows + c, :] = rows
        out_ref[:, 2 * cap_rows + 3, c * looks : (c + 1) * looks] = side
    out_ref[:, 2 * cap_rows + 2, :] = rim_ref[...]
    out_ref[:, 2 * cap_rows + 3, 2 * looks : 3 * looks] = side_ref[...]


def prepare_kernel(cap_rows, table_rows, slots, width, map_lat, got_ref, hot_ref, row_ref, sum_ref):
    tiles = got_ref.shape[0]
    packed = LANES // width
    lane = lane_iota((1, LANES))
    for t in range(tiles):
        for k in range(cap_rows):
            def channel(c):
                return got_ref[t, table_rows + c * cap_rows + k : table_rows + c * cap_rows + k + 1, :]

            cell = None
            for i in range(packed):
                place, spot = divmod(3 * slots + k * packed + i, table_rows)
                x = roll(got_ref[t, spot : spot + 1, :], (i - place) * width, 1)
                cell = x if cell is None else jnp.where(lane // width == i, x, cell)
            cell = cell.astype(I32)
            line, column = jnp.right_shift(cell, LANES.bit_length() - 1), jnp.bitwise_and(cell, LANES - 1)
            at = (t * cap_rows + k) * LANES
            cut = slice(at, at + LANES)
            hot_ref[:, cut] = (row_iota((LANES, LANES)) == column).astype(F32).astype(BF16)
            rows = row_iota((map_lat, LANES))
            here, next_line = rows == line, rows == line + 1
            for d in range(2):
                row_ref[d * map_lat : (d + 1) * map_lat, cut] = jnp.where(here, channel(d), 0.0) + jnp.where(
                    next_line, channel(2 + d), 0.0
                )
    high, low = split(row_ref[...])
    acc = dot_nt(high, hot_ref[...]) + dot_nt(low, hot_ref[...])
    shifted = roll(acc[map_lat:], 1, 1)
    total = acc[:map_lat] + jnp.where(lane_iota(shifted.shape) == 0, 0.0, shifted)
    sum_ref[...] = total


def splat_kernel(cap_rows, map_lat, got_ref, hot_ref, row_ref, weight_ref, out_ref, x_ref):
    tiles = got_ref.shape[0]
    wide = 2 * map_lat
    for t in range(tiles):
        for k in range(cap_rows):
            cut = slice((t * cap_rows + k) * LANES, (t * cap_rows + k + 1) * LANES)
            for c in range(2):
                value = got_ref[t, c * cap_rows + k : c * cap_rows + k + 1, :]
                high, low = split(row_ref[:, cut] * value)
                x_ref[c * wide : (c + 1) * wide, cut] = high
                x_ref[(2 + c) * wide : (3 + c) * wide, cut] = low
    acc = dot_nt(x_ref[...], hot_ref[...])
    acc = acc[: 2 * wide] + acc[2 * wide :]
    edges = got_ref[0]
    for t in range(1, tiles):
        edges = edges + got_ref[t]
    weight = jnp.maximum(add_edges(weight_ref[...], edges, 2, 2 * cap_rows), 1.0)
    for c in range(2):
        shifted = roll(acc[c * wide + map_lat : (c + 1) * wide], 1, 1)
        total = acc[c * wide : c * wide + map_lat] + jnp.where(lane_iota(shifted.shape) == 0, 0.0, shifted)
        out_ref[c] = add_edges(total, edges, c, 2 * cap_rows) / weight


def filter_constants(block_rows):
    az, rg, back, last = filter_tables(block_rows)
    az_h, az_l = host_split(az)
    rg_h, rg_l = host_split(rg)
    back_h, back_l = host_split(back)
    last_h, last_l = host_split(last)
    zero = np.zeros_like(back_l)
    back = np.concatenate([np.concatenate([back_h, back_h], axis=1), np.concatenate([back_l, zero], axis=1)], axis=0)
    final = np.zeros((2 * PATCH, rg_h.shape[1]), BF16)
    final[:, : 6 * HALF] = np.concatenate([az_h, az_h, az_l], axis=1)
    final[: back.shape[0], 2 * LANES : 2 * LANES + back.shape[1]] = back
    return np.concatenate([rg_h, rg_l, np.concatenate([last_h, last_l], axis=1), final], axis=0)


def filter_scratch(rows, samples, block_rows, map_lat, map_lon, tiles):
    patches = samples // STEP
    count = block_rows * PATCH
    return (
        VMEM((6 * HALF, rows // HALF * (samples + LANES)), BF16),
        VMEM((patches + 1, count, 2 * PATCH), F32),
        VMEM((patches, count, 2 * PATCH), F32),
        VMEM((patches, block_rows, 8, LANES), F32),
        VMEM((2 * count, patches * LANES), BF16),
        VMEM((2, map_lat, map_lon), F32),
        VMEM((16 * tiles, map_lat * map_lon), BF16),
    )


def swap_pairs(count, first):
    return [p for i in range(first, count - 1, 2) for p in ((i, i + 1), (i + 1, i))]


def body(image, factor, heights, listing, position, owner, base, shares):
    n_az, n_rg = lax.axis_size("az"), lax.axis_size("rg")
    tiles = n_az * n_rg
    both = ("az", "rg")
    lats, lons, points = heights.shape
    slots = listing.shape[1]
    width = points // tiles
    packed = LANES // width
    lines, samples = factor.shape
    map_lat, map_lon = lines // LOOK, samples // LOOK
    block_rows = lines // STEP
    capacity = 2 * map_lat * map_lon // tiles
    cap_rows = -(-capacity // LANES)
    table_rows = -(-(3 * slots + cap_rows * packed) // packed)
    table_rows = -(-table_rows // 8) * 8
    early_rows = 4 * cap_rows
    late_rows = -(-(2 * cap_rows + 4) // 8) * 8
    slice_rows = lats * lons // packed
    parity = (lax.axis_index("az") % 2).astype(I32).reshape(1)
    rg = lax.axis_index("rg").astype(I32).reshape(1)

    def exchange(x):
        return lax.all_to_all(x, both, split_axis=0, concat_axis=0, tiled=True)

    slices = call(
        functools.partial(slice_kernel, width),
        sds((tiles, slice_rows + 8, LANES)),
        (heights, listing),
        grant=60,
    )
    got_slices = exchange(slices)
    one, two = call(halo_kernel, [sds((4, RIM, samples))] * 2, (parity, image, factor, position), smem=(0,))
    one = lax.ppermute(one, "az", swap_pairs(n_az, 0))
    two = lax.ppermute(two, "az", swap_pairs(n_az, 1))
    total = map_lat * map_lon
    looks_at = (owner.reshape(map_lat, map_lon), base.reshape(map_lat, map_lon), shares.reshape(4, map_lat, map_lon))
    early, cells, rim_sum, side_sum, at_m, at_n, *edges = call(
        functools.partial(pack_kernel, n_rg, cap_rows),
        [
            sds((tiles, early_rows, LANES)),
            sds((tiles, cap_rows * LANES)),
            sds((tiles, map_lon)),
            sds((tiles, map_lat)),
            sds((tiles, cap_rows * LANES), I32),
            sds((tiles, cap_rows * LANES), I32),
            sds((map_lon, total), BF16),
            sds((map_lat, total), BF16),
            sds((map_lat, total), BF16),
        ],
        looks_at,
        scratch=(VMEM((cap_rows * LANES, total), BF16), VMEM((3 * tiles, total), BF16), VMEM((8 * tiles, total), BF16)),
    )
    got_slices, early, one, two = lax.optimization_barrier((got_slices, early, one, two))
    request = call(
        functools.partial(request_kernel, n_rg, (lats, lons), width, table_rows, slots),
        sds((tiles, table_rows + early_rows, LANES)),
        (got_slices, early, cells),
        scratch=(
            VMEM((packed, tiles * (slice_rows + 8), LANES), F32),
            VMEM((2, tiles, LANES), I32),
            pltpu.SMEM((2, tiles, LANES), I32),
            pltpu.SemaphoreType.DMA((1,)),
        ),
    )
    tables = exchange(request)
    flat, edge = call(
        functools.partial(flatten_kernel, width, table_rows, slots),
        [sds((2, lines + 2 * RIM, samples)), sds((2, lines + 2 * RIM, LANES))],
        (parity, tables, image, factor, position, one, two),
        smem=(0,),
        scratch=(
            VMEM((tiles // packed, packed * table_rows, LANES), F32),
            VMEM((3, lines + 2 * RIM, samples), F32),
            VMEM((lines + 2 * RIM, samples), I32),
        ),
    )
    edge = lax.ppermute(edge, "rg", swap_pairs(n_rg, 0))
    rows = lines + 2 * RIM
    patches = samples // STEP
    count = block_rows * PATCH
    packed_looks = call(
        functools.partial(filter_kernel, n_rg, cap_rows, block_rows),
        sds((tiles, late_rows, LANES)),
        (rg, flat, edge, rim_sum, side_sum, at_m, at_n, *looks_at, filter_constants(block_rows), *edges),
        smem=(0,),
        scratch=filter_scratch(rows, samples, block_rows, map_lat, map_lon, tiles),
    )
    got = exchange(packed_looks)
    wide = tiles * cap_rows * LANES
    hot, row_weights, weight_sum = call(
        functools.partial(prepare_kernel, cap_rows, table_rows, slots, width, map_lat),
        [sds((LANES, wide), BF16), sds((2 * map_lat, wide)), sds((map_lat, map_lon))],
        (tables,),
    )
    return call(
        functools.partial(splat_kernel, cap_rows, map_lat),
        sds((2, map_lat, map_lon)),
        (got, hot, row_weights, weight_sum),
        scratch=(VMEM((8 * map_lat, wide), BF16),),
    )


def solution(mesh):
    return jax.shard_map(
        body,
        mesh=mesh,
        in_specs=(
            P(None, ("scene", "az"), "rg"),
            P(("scene", "az"), "rg"),
            P(("scene", "az"), "rg", None),
            P(("scene", "az", "rg"), None),
            P(("scene", "az"), "rg"),
            P(("scene", "az", "rg"), None),
            P(("scene", "az", "rg")),
            P(None, ("scene", "az", "rg")),
        ),
        out_specs=P(None, ("scene", "az"), "rg"),
        check_vma=False,
    )
```

```python
import functools
import math

import jax
import jax.numpy as jnp
import numpy as np
from jax import lax
from jax.experimental import pallas as pl
from jax.experimental.pallas import tpu as pltpu
from jax.sharding import PartitionSpec as P


PATCH = 64
LOOK = 4
EPS = 1e-06
LANES = 128
RIM = PATCH // 4
STEP = PATCH // 2
HALF = PATCH // 2
F32 = jnp.float32
BF16 = jnp.bfloat16
I32 = jnp.int32
VMEM = pltpu.VMEM
VSPEC = pl.BlockSpec(memory_space=pltpu.VMEM)
SSPEC = pl.BlockSpec(memory_space=pltpu.SMEM)


def call(kernel, outs, args, scratch=(), smem=(), grant=16, cost=(1_000_000, 1_000_000)):
    return pl.pallas_call(
        kernel,
        out_shape=outs,
        in_specs=[SSPEC if i in smem else VSPEC for i in range(len(args))],
        out_specs=jax.tree.map(lambda _: VSPEC, outs),
        scratch_shapes=list(scratch),
        compiler_params=pltpu.CompilerParams(vmem_limit_bytes=grant << 20),
        cost_estimate=pl.CostEstimate(flops=cost[0], bytes_accessed=cost[1], transcendentals=0),
    )(*args)


def sds(shape, dtype=F32):
    return jax.ShapeDtypeStruct(shape, dtype)


def split(x):
    hi = x.astype(BF16)
    return hi, (x - hi.astype(F32)).astype(BF16)


def dot(a, b):
    return jnp.dot(a, b, preferred_element_type=F32)


def dot_nt(a, b):
    return lax.dot_general(a, b, (((1,), (1,)), ((), ())), preferred_element_type=F32)


def fetch(pairs, sems):
    copies = [pltpu.make_async_copy(src, dst, sems.at[i]) for i, (src, dst) in enumerate(pairs)]
    for copy in copies:
        copy.start()
    return copies


def lane_iota(shape):
    return lax.broadcasted_iota(I32, shape, len(shape) - 1)


def row_iota(shape):
    return lax.broadcasted_iota(I32, shape, 0)


def roll(x, shift, axis):
    shift = shift % x.shape[axis]
    return x if shift == 0 else pltpu.roll(x, shift, axis)


def lane_gather(row, index):
    return jnp.take_along_axis(jnp.broadcast_to(row, index.shape), index, axis=1)


def host_split(x):
    hi = np.asarray(x, np.float32).astype(BF16)
    lo = (np.asarray(x, np.float64) - hi.astype(np.float64)).astype(BF16)
    return hi, lo


UNROLL = 4


def filter_tables(block_rows):
    turn = 2.0 * math.pi / PATCH
    step = np.arange(PATCH)
    cosine = np.cos(turn * (step[:, None] * step[None, :] % PATCH))
    sine = np.sin(turn * (step[:, None] * step[None, :] % PATCH))
    count = block_rows * PATCH
    az = np.zeros((2 * PATCH, 2 * HALF))
    az[:PATCH, :HALF], az[:PATCH, HALF:] = cosine[:, :HALF], sine[:, :HALF]
    az[PATCH:, :HALF], az[PATCH:, HALF:] = -sine[:, :HALF], cosine[:, :HALF]
    rg = np.zeros((2 * LANES, 4 * PATCH))
    for p in range(2):
        w, wi = slice(p * HALF, p * HALF + PATCH), slice(LANES + p * HALF, LANES + p * HALF + PATCH)
        lr, li = slice(p * PATCH, (p + 1) * PATCH), slice(LANES + p * PATCH, LANES + (p + 1) * PATCH)
        rg[w, lr], rg[wi, lr] = cosine, sine
        rg[w, li], rg[wi, li] = -sine, cosine
    looks = STEP // LOOK
    core = cosine[RIM : RIM + STEP].reshape(looks, LOOK, PATCH).mean(axis=1)
    core_s = sine[RIM : RIM + STEP].reshape(looks, LOOK, PATCH).mean(axis=1)
    back = np.zeros((2 * block_rows * looks, count))
    for u in range(block_rows):
        k = slice(u * PATCH, (u + 1) * PATCH)
        back[u * looks : (u + 1) * looks, k] = core / PATCH
        back[(block_rows + u) * looks : (block_rows + u + 1) * looks, k] = core_s / PATCH
    c_l, s_l = core.T / PATCH, core_s.T / PATCH
    reps = LANES // looks
    patch_of = np.arange(LANES) // looks % 2
    last = np.zeros((4 * LANES, 2 * LANES))
    terms = ((c_l, s_l), (-s_l, c_l), (-s_l, c_l), (-c_l, -s_l))
    for i, (re, im) in enumerate(terms):
        for p in range(2):
            k = slice(i * LANES + p * PATCH, i * LANES + (p + 1) * PATCH)
            last[k, :LANES] = np.tile(re, reps) * (patch_of == p)
            last[k, LANES:] = np.tile(im, reps) * (patch_of == p)
    return az, rg, back, last


def slice_kernel(width, dem_ref, list_ref, out_ref):
    tiles = out_ref.shape[0]
    lats, lons, _ = dem_ref.shape
    packed = LANES // width
    groups = lats // packed
    slots = list_ref.shape[1]
    lane = lane_iota((lons, LANES))
    listed = list_ref[...].astype(F32)
    for q in range(tiles):
        tile, offset = divmod(q * width, LANES)
        for g in range(groups):
            total = None
            for p in range(packed):
                x = dem_ref[p * groups + g, :, tile * LANES : (tile + 1) * LANES]
                x = roll(x, p * width - offset, 1)
                total = x if total is None else jnp.where(lane // width == p, x, total)
            out_ref[q, g * lons : (g + 1) * lons, :] = total
        out_ref[q, groups * lons : groups * lons + 1, 0:slots] = listed


def halo_kernel(par_ref, image_ref, factor_ref, position_ref, one_ref, two_ref):
    even = par_ref[0] == 0
    lines = factor_ref.shape[0]
    fields = (
        lambda s: image_ref[0, s, :],
        lambda s: image_ref[1, s, :],
        lambda s: factor_ref[s, :],
        lambda s: position_ref[s, :].astype(F32),
    )
    for i, field in enumerate(fields):
        first = field(slice(0, RIM))
        last = field(slice(lines - RIM, lines))
        one_ref[i] = jnp.where(even, last, first)
        two_ref[i] = jnp.where(even, first, last)


def border_sums(n_rg, tiles, values, owner_ref, base_ref, share_ref, w_ref, term_ref, col_ref, here_ref, next_ref):
    channels = len(values)
    height, width = owner_ref.shape
    base = base_ref[...]
    last_line = jnp.right_shift(base, width.bit_length() - 1) == height - 1
    last_column = jnp.bitwise_and(base, width - 1) == width - 1
    owner = owner_ref[...]
    on_line = jnp.where(last_line, owner, -1)
    on_column = jnp.where(last_column, owner, -1)
    terms = []
    for c, value in enumerate(values):
        for i in range(2):
            spot = (i * channels + c) * tiles
            far = 4 * channels * tiles + spot
            for mask, k, row in ((0, 2, 2 * spot), (0, 3, 2 * spot + tiles), (1, 1, far), (1, 3, far + 2 * channels * tiles)):
                x = share_ref[k] if value is None else share_ref[k] * value
                high = x.astype(BF16).astype(F32)
                term_ref[len(terms)] = high if i == 0 else x - high
                terms.append((mask, row))
    tile = row_iota((tiles, width))
    for m in range(height):
        cut = slice(m * width, (m + 1) * width)
        masks = (tile == on_line[m : m + 1], tile == on_column[m : m + 1])
        for n, (mask, row) in enumerate(terms):
            w_ref[row : row + tiles, cut] = jnp.where(masks[mask], term_ref[n, m : m + 1, :], 0.0).astype(BF16)
    size = channels * tiles
    b = dot_nt(w_ref[0 : 4 * size], col_ref[...])
    b = b[: 2 * size] + b[2 * size :]
    side = dot_nt(w_ref[4 * size : 6 * size], here_ref[...]) + dot_nt(w_ref[6 * size : 8 * size], next_ref[...])
    side = side[:size] + side[size:]
    results = []
    for c in range(channels):
        b0, b1 = b[2 * c * tiles : (2 * c + 1) * tiles], b[(2 * c + 1) * tiles : (2 * c + 2) * tiles]
        dest = row_iota(b0.shape)
        shifted = roll(b1, 1, 1)
        below = roll(b0, n_rg, 0)
        beside = roll(shifted, n_rg, 0)
        diagonal = jnp.where(dest % n_rg > 0, roll(shifted, n_rg + 1, 0), 0.0)
        beside = jnp.where(lane_iota(b0.shape) == 0, diagonal, beside)
        rows = jnp.where(dest >= n_rg, below + beside, 0.0)
        one = side[c * tiles : (c + 1) * tiles]
        one = jnp.concatenate([jnp.zeros((1, one.shape[1]), F32), one[:-1]], axis=0)
        results.append((rows, jnp.where(row_iota(one.shape) % n_rg > 0, one, 0.0)))
    return results


def add_edges(total, edges, channel, first):
    rows, lanes = row_iota(total.shape), lane_iota(total.shape)
    edge, side = edges[first + channel : first + channel + 1], edges[first + 3 : first + 4]
    column = jnp.sum(jnp.where(lanes == rows + channel * total.shape[0], side, 0.0), axis=1, keepdims=True)
    return total + jnp.where(rows == 0, edge, 0.0) + jnp.where(lanes == 0, column, 0.0)


def pack_kernel(n_rg, cap_rows, owner_ref, base_ref, share_ref, early_ref, cell_ref, rim_ref, side_ref, im_ref, in_ref, col_ref, here_ref, next_ref, hot_ref, lhs_ref, w_ref, term_ref):
    tiles = early_ref.shape[0]
    height, width = owner_ref.shape
    owner = owner_ref[...]
    batch = min(tiles, 16)
    tri = (row_iota((width, width)) < lane_iota((width, width))).astype(BF16)
    ones = jnp.ones((width, width), BF16)
    size = batch * height
    r, c = row_iota((size, size)), lane_iota((size, size))
    lower = ((r // height == c // height) & (c < r)).astype(BF16)
    rank = jnp.zeros((height, width), F32)
    for b in range(tiles // batch):
        hot = jnp.concatenate([(owner == b * batch + o).astype(F32) for o in range(batch)], axis=0)
        hot16 = hot.astype(BF16)
        before = dot(hot16, tri) + dot(lower, dot(hot16, ones).astype(BF16))
        kept = hot * before
        for o in range(batch):
            rank = rank + kept[o * height : (o + 1) * height]
    rank = rank.astype(I32)
    base = base_ref[...]
    shift = width.bit_length() - 1
    column = jnp.bitwise_and(base, width - 1)
    line = jnp.right_shift(base, shift)
    cap = cap_rows * LANES
    for m in range(height):
        cut = slice(m * width, (m + 1) * width)
        hot_ref[:, cut] = (row_iota((cap, width)) == rank[m : m + 1]).astype(F32).astype(BF16)
        col_ref[:, cut] = (row_iota((width, width)) == column[m : m + 1]).astype(F32).astype(BF16)
        mine = row_iota((tiles, width)) == owner[m : m + 1]
        lhs_ref[0:tiles, cut] = mine.astype(F32).astype(BF16)
        lhs_ref[tiles : 2 * tiles, cut] = jnp.where(mine, float(m), 0.0).astype(BF16)
        lhs_ref[2 * tiles :, cut] = jnp.where(mine, lane_iota((tiles, width)).astype(F32), 0.0).astype(BF16)
        at = row_iota((height, width))
        here_ref[:, cut] = (at == line[m : m + 1]).astype(F32).astype(BF16)
        next_ref[:, cut] = (at == line[m : m + 1] + 1).astype(F32).astype(BF16)
    found = dot_nt(lhs_ref[...], hot_ref[...])
    valid = found[0:tiles] > 0.5
    at_m = found[tiles : 2 * tiles].astype(I32)
    at_n = found[2 * tiles :].astype(I32)
    im_ref[...] = at_m
    in_ref[...] = at_n
    cell = base.astype(F32)
    for channel in range(5):
        for k in range(cap_rows):
            cut = slice(k * LANES, (k + 1) * LANES)
            total = jnp.zeros((tiles, LANES), F32)
            for m in range(height):
                row = cell[m : m + 1] if channel == 4 else share_ref[channel, m : m + 1, :]
                total = jnp.where(at_m[:, cut] == m, lane_gather(row, at_n[:, cut]), total)
            total = jnp.where(valid[:, cut], total, 0.0)
            if channel == 4:
                cell_ref[:, cut] = total
            else:
                early_ref[:, channel * cap_rows + k, :] = total
    ((rows, side),) = border_sums(n_rg, tiles, [None], owner_ref, base_ref, share_ref, w_ref, term_ref, col_ref, here_ref, next_ref)
    rim_ref[...] = rows
    side_ref[...] = side


def request_kernel(n_rg, grid, width, table_rows, slots, got_ref, early_ref, cell_ref, out_ref, turn_ref, list_ref, index_ref, sem):
    tiles, rows, _ = got_ref.shape
    lats, lons = grid
    packed = LANES // width
    groups = lats // packed
    listed = jnp.maximum(got_ref[:, rows - 8, :], 0.0)
    listed = jnp.where(lane_iota(listed.shape) < slots, listed, 0.0).astype(I32)
    lat, lon = listed // (lons * n_rg), listed % (lons * n_rg)
    key = lat // lats * n_rg + lon // lons
    list_ref[0] = key * rows + lat % lats % groups * lons + lon % lons
    list_ref[1] = lat % lats // groups
    (copy,) = fetch(((list_ref, index_ref),), sem)
    for t in range(tiles):
        x = got_ref[t]
        for p in range(packed):
            turn_ref[p, t * rows : (t + 1) * rows, :] = roll(x, p * width, 1)
        out_ref[t, table_rows:, :] = early_ref[t]
    for k in range(cell_ref.shape[1] // LANES):
        x = cell_ref[:, k * LANES : (k + 1) * LANES]
        for i in range(packed):
            place, line = divmod(3 * slots + k * packed + i, table_rows)
            cut = slice(place * width, (place + 1) * width)
            out_ref[:, line, cut] = roll(x, (place - i) * width, 1)[:, cut]
    copy.wait()
    for t in range(tiles):
        for f in range(slots):
            row, piece = index_ref[0, t, f], index_ref[1, t, f]
            for n, dest in ((0, t + n_rg), (1, t), (2, t - n_rg)):
                if 0 <= dest < tiles:
                    place, line = divmod(n * slots + f, table_rows)
                    turn = jnp.bitwise_and(place - piece, packed - 1)
                    put = turn_ref[turn, pl.ds(row, 1), :]
                    cut = slice(place * width, (place + 1) * width)
                    out_ref[dest, line : line + 1, cut] = put[:, cut]


def sincos(x):
    n = jnp.floor(x * (2.0 / math.pi) + 0.5)
    r = x - n * 1.5703125
    r = r - n * 4.837512969970703e-4
    r = r - n * 7.549789954891882e-8
    z = r * r
    s = ((-1.9515295891e-4 * z + 8.3321608736e-3) * z - 1.6666654611e-1) * z * r + r
    c = ((2.443315711809948e-5 * z - 1.388731625493765e-3) * z + 4.166664568298827e-2) * z * z - 0.5 * z + 1.0
    q = n.astype(I32)
    odd = (q & 1) == 1
    sine = jnp.where(odd, c, s)
    cosine = jnp.where(odd, s, c)
    sine = jnp.where((q & 2) == 2, -sine, sine)
    cosine = jnp.where(((q + 1) & 2) == 2, -cosine, cosine)
    return cosine, sine


def flatten_kernel(width, table_rows, slots, par_ref, got_ref, image_ref, factor_ref, position_ref, one_ref, two_ref, flat_ref, edge_ref, tab_ref, in_ref, at_ref):
    even = par_ref[0] == 0
    lines, samples = factor_ref.shape
    packed = LANES // width
    tiles = got_ref.shape[0]
    parts = tiles // packed
    lane = lane_iota((table_rows, LANES))
    for k in range(parts):
        for place in range(packed):
            total = None
            for j in range(packed):
                x = roll(got_ref[k * packed + j, 0:table_rows, :], (j - place) * width, 1)
                total = x if total is None else jnp.where(lane // width == j, x, total)
            tab_ref[k, place * table_rows : (place + 1) * table_rows, :] = total
    for i in range(3):
        top = jnp.where(even, two_ref[i], one_ref[i])
        low = jnp.where(even, one_ref[i], two_ref[i])
        in_ref[i, 0:RIM] = top
        in_ref[i, RIM + lines :] = low
    in_ref[0, RIM : RIM + lines] = image_ref[0]
    in_ref[1, RIM : RIM + lines] = image_ref[1]
    in_ref[2, RIM : RIM + lines] = factor_ref[...]
    at_ref[0:RIM] = jnp.where(even, two_ref[3], one_ref[3]).astype(I32)
    at_ref[RIM : RIM + lines] = position_ref[...]
    at_ref[RIM + lines :] = jnp.where(even, one_ref[3], two_ref[3]).astype(I32)
    W = 1
    cols = samples // LANES
    shift = LANES.bit_length() - 1
    part_bits = parts.bit_length() - 1
    groups = (lines + 2 * RIM) // 8
    steps = groups * cols // W
    rim_steps = RIM // 8 * cols // W

    def step(i):
        base = jnp.where(i < rim_steps, 0, jnp.where(i < steps - rim_steps, slots, 2 * slots))
        spots = []
        for j in range(W):
            n = i * W + j
            if W >= cols:
                spots.append((pl.ds(pl.multiple_of((i * (W // cols) + j // cols) * 8, 8), 8), pl.ds(j % cols * LANES, LANES)))
            else:
                spots.append((pl.ds(pl.multiple_of(n // cols * 8, 8), 8), pl.ds(pl.multiple_of(n % cols * LANES, LANES), LANES)))
        at = [at_ref[spot] for spot in spots]
        lanes = [jnp.bitwise_and(x, LANES - 1) for x in at]
        bits = [[jnp.bitwise_and(x, LANES << b) != 0 for b in range(part_bits)] for x in at]
        slot = [jnp.right_shift(x, shift + part_bits) for x in at]
        height = [None] * W
        for f in range(slots):
            rows = [jnp.broadcast_to(tab_ref[k, pl.ds(base + f, 1), :], (8, LANES)) for k in range(parts)]
            for j in range(W):
                x = [jnp.take_along_axis(row, lanes[j], axis=1) for row in rows]
                for b in range(part_bits):
                    x = [jnp.where(bits[j][b], x[n + 1], x[n]) for n in range(0, len(x), 2)]
                height[j] = x[0] if f == 0 else jnp.where(slot[j] == f, x[0], height[j])
        for spot, h in zip(spots, height):
            cosine, sine = sincos(in_ref[(2, *spot)] * h)
            a, b = in_ref[(0, *spot)], in_ref[(1, *spot)]
            flat_ref[(0, *spot)] = a * cosine + b * sine
            flat_ref[(1, *spot)] = b * cosine - a * sine

    pl.loop(0, steps, unroll=16)(step)
    edge = lane_iota((lines + 2 * RIM, LANES))
    for c in range(2):
        first = flat_ref[c, :, 0:LANES]
        last = roll(flat_ref[c, :, samples - LANES : samples], 2 * RIM, 1)
        edge_ref[c] = jnp.where(edge < RIM, first, jnp.where(edge < 2 * RIM, last, 0.0))


def root(x):
    return x * lax.rsqrt(jnp.maximum(x, 1e-37))


def filter_kernel(n_rg, cap_rows, block_rows, rg_ref, flat_ref, edge_ref, rim_ref, side_ref, im_ref, in_ref, owner_ref, base_ref, share_ref, const_ref, col_ref, here_ref, next_ref, out_ref, x_ref, y_ref, m_ref, s_ref, p_ref, z_ref, look_ref, w_ref, term_ref):
    _, rows, samples = flat_ref.shape
    cols = samples // LANES
    wide = (cols + 1) * LANES
    lane = lane_iota((HALF, LANES))
    left = rg_ref[0] > 0
    right = rg_ref[0] < n_rg - 1
    strips = rows // HALF
    for p in range(strips):
        for c in range(2):
            cut = slice(p * HALF, (p + 1) * HALF)
            halo = edge_ref[c, cut]
            before = jnp.where(left, roll(halo, -RIM, 1), 0.0)
            after = jnp.where(right, roll(halo, RIM, 1), 0.0)
            for j in range(cols + 1):
                if j < cols:
                    now = roll(flat_ref[c, cut, j * LANES : (j + 1) * LANES], RIM, 1)
                else:
                    now = jnp.where(lane < 2 * RIM, after, 0.0)
                high, low = split(jnp.where(lane < RIM, before, now))
                before = now
                at = slice(p * wide + j * LANES, p * wide + (j + 1) * LANES)
                x_ref[c * HALF : (c + 1) * HALF, at] = high
                x_ref[(2 + c) * HALF : (3 + c) * HALF, at] = low
                x_ref[(4 + c) * HALF : (5 + c) * HALF, at] = high
    looks = block_rows * STEP // LOOK
    block = const_ref[...]

    def tripled(at, size):
        return jnp.concatenate([block[at : at + size], block[at : at + size], block[at + size : at + 2 * size]], axis=0)

    rg3 = tripled(0, 2 * LANES)
    last3 = tripled(4 * LANES, 4 * LANES)
    near = jnp.concatenate([block[12 * LANES : 13 * LANES, :LANES]] * 2, axis=0)
    side = jnp.concatenate([block[12 * LANES : 13 * LANES, LANES:]] * 2, axis=0)
    az = block[13 * LANES : 13 * LANES + 2 * PATCH, : 6 * HALF]
    back = block[14 * LANES : 14 * LANES + 4 * looks, : 2 * block_rows * PATCH]
    e = dot(az, x_ref[...])
    count = block_rows * PATCH
    flip = jnp.where(row_iota((PATCH, LANES)) % 2 == 0, 1.0, -1.0)
    half = lane_iota((count, LANES)) < PATCH

    def spectrum(c, j):
        cells = []
        for u in range(block_rows):
            one = e[c * PATCH : (c + 1) * PATCH, u * wide + j * LANES : u * wide + (j + 1) * LANES]
            two = e[c * PATCH : (c + 1) * PATCH, (u + 1) * wide + j * LANES : (u + 1) * wide + (j + 1) * LANES]
            cells.append(one + flip * two)
        return jnp.concatenate(cells, axis=0)

    parts = []
    for c in range(2):
        cells = [spectrum(c, j) for j in range(cols + 1)]
        turned = [pltpu.roll(x, PATCH, 1) for x in cells]
        windows = []
        for j in range(cols):
            windows += [cells[j], jnp.where(half, turned[j], turned[j + 1])]
        parts.append(split(jnp.concatenate(windows, axis=0)))
    (rh, rl), (ih, il) = parts
    y_ref[...] = dot(jnp.concatenate([rh, ih, rl, il, rh, ih], axis=1), rg3)
    pairs = 2 * cols

    def measure(w):
        at = pl.multiple_of(w * count, count)
        re, im = y_ref[pl.ds(at, count), :LANES], y_ref[pl.ds(at, count), LANES:]
        magnitude = root(re * re + im * im)
        high, low = split(magnitude)
        m_ref[pl.ds(at, count), :LANES] = high
        m_ref[pl.ds(at, count), LANES:] = low
        for u in range(block_rows):
            part = magnitude[u * PATCH : u * PATCH + 8]
            for i in range(1, PATCH // 8):
                part = part + magnitude[u * PATCH + 8 * i : u * PATCH + 8 * i + 8]
            p_ref[pl.ds(pl.multiple_of((w * block_rows + u) * 8, 8), 8), :] = part

    pl.loop(0, pairs, unroll=UNROLL)(measure)
    s_ref[...] = dot(m_ref[...], near)
    ph, plow = split(p_ref[...])
    sums = dot(jnp.concatenate([ph, plow], axis=1), side)
    for n in range(pairs * block_rows):
        x = sums[8 * n : 8 * n + 8]
        for shift in (4, 2, 1):
            x = x + pltpu.roll(x, shift, 0)
        p_ref[8 * n : 8 * n + 8, :] = 1.0 / (9.0 * (x * (1.0 / (PATCH * PATCH)) + EPS))

    def weigh(w):
        at = pl.multiple_of(w * 2 * LANES, 2 * LANES)
        for u in range(block_rows):
            cut = pl.ds(pl.multiple_of(w * count + u * PATCH, PATCH), PATCH)
            su = s_ref[cut, :]
            su = su + pltpu.roll(su, 1, 0) + pltpu.roll(su, PATCH - 1, 0)
            factor = p_ref[pl.ds(pl.multiple_of((w * block_rows + u) * 8, 8), 8), :]
            gain = root(su * jnp.concatenate([factor] * (PATCH // 8), axis=0))
            for c in range(2):
                high, low = split(y_ref[cut, c * LANES : (c + 1) * LANES] * gain)
                span = pl.ds(pl.multiple_of(at + c * LANES, LANES), LANES)
                z_ref[u * PATCH : (u + 1) * PATCH, span] = high
                z_ref[count + u * PATCH : count + (u + 1) * PATCH, span] = low

    pl.loop(0, pairs, unroll=UNROLL)(weigh)
    t = dot(back, z_ref[...])
    t = t[: 2 * looks] + t[2 * looks :]
    stacked = jnp.concatenate(
        [
            jnp.concatenate([t[i * looks : (i + 1) * looks, w * 2 * LANES : (w + 1) * 2 * LANES] for i in range(2)], axis=1)
            for w in range(pairs)
        ],
        axis=0,
    )
    sh, sl = split(stacked)
    y = dot(jnp.concatenate([sh, sl, sh], axis=1), last3)
    group = lane_iota((looks, LANES)) // (2 * STEP // LOOK)
    for c in range(2):
        total = jnp.zeros((looks, LANES), F32)
        for w in range(pairs):
            total = jnp.where(group == w, y[w * looks : (w + 1) * looks, c * LANES : (c + 1) * LANES], total)
        look_ref[c] = total
    tiles = out_ref.shape[0]
    for k in range(cap_rows):
        cut = slice(k * LANES, (k + 1) * LANES)
        at_m, at_n = im_ref[:, cut], in_ref[:, cut]
        for c in range(2):
            total = jnp.zeros((tiles, LANES), F32)
            for m in range(looks):
                total = jnp.where(at_m == m, lane_gather(look_ref[c, m : m + 1, :], at_n), total)
            out_ref[:, c * cap_rows + k, :] = total
    values = [look_ref[0], look_ref[1]]
    borders = border_sums(n_rg, tiles, values, owner_ref, base_ref, share_ref, w_ref, term_ref, col_ref, here_ref, next_ref)
    for c, (rows, side) in enumerate(borders):
        out_ref[:, 2 * cap_rows + c, :] = rows
        out_ref[:, 2 * cap_rows + 3, c * looks : (c + 1) * looks] = side
    out_ref[:, 2 * cap_rows + 2, :] = rim_ref[...]
    out_ref[:, 2 * cap_rows + 3, 2 * looks : 3 * looks] = side_ref[...]


def prepare_kernel(cap_rows, table_rows, slots, width, map_lat, got_ref, hot_ref, row_ref, sum_ref):
    tiles = got_ref.shape[0]
    packed = LANES // width
    lane = lane_iota((1, LANES))
    for t in range(tiles):
        for k in range(cap_rows):
            def channel(c):
                return got_ref[t, table_rows + c * cap_rows + k : table_rows + c * cap_rows + k + 1, :]

            cell = None
            for i in range(packed):
                place, spot = divmod(3 * slots + k * packed + i, table_rows)
                x = roll(got_ref[t, spot : spot + 1, :], (i - place) * width, 1)
                cell = x if cell is None else jnp.where(lane // width == i, x, cell)
            cell = cell.astype(I32)
            line, column = jnp.right_shift(cell, LANES.bit_length() - 1), jnp.bitwise_and(cell, LANES - 1)
            at = (t * cap_rows + k) * LANES
            cut = slice(at, at + LANES)
            hot_ref[:, cut] = (row_iota((LANES, LANES)) == column).astype(F32).astype(BF16)
            rows = row_iota((map_lat, LANES))
            here, next_line = rows == line, rows == line + 1
            for d in range(2):
                row_ref[d * map_lat : (d + 1) * map_lat, cut] = jnp.where(here, channel(d), 0.0) + jnp.where(
                    next_line, channel(2 + d), 0.0
                )
    high, low = split(row_ref[...])
    acc = dot_nt(high, hot_ref[...]) + dot_nt(low, hot_ref[...])
    shifted = roll(acc[map_lat:], 1, 1)
    total = acc[:map_lat] + jnp.where(lane_iota(shifted.shape) == 0, 0.0, shifted)
    sum_ref[...] = total


def splat_kernel(cap_rows, map_lat, got_ref, hot_ref, row_ref, weight_ref, out_ref, x_ref):
    tiles = got_ref.shape[0]
    wide = 2 * map_lat
    for t in range(tiles):
        for k in range(cap_rows):
            cut = slice((t * cap_rows + k) * LANES, (t * cap_rows + k + 1) * LANES)
            for c in range(2):
                value = got_ref[t, c * cap_rows + k : c * cap_rows + k + 1, :]
                high, low = split(row_ref[:, cut] * value)
                x_ref[c * wide : (c + 1) * wide, cut] = high
                x_ref[(2 + c) * wide : (3 + c) * wide, cut] = low
    acc = dot_nt(x_ref[...], hot_ref[...])
    acc = acc[: 2 * wide] + acc[2 * wide :]
    edges = got_ref[0]
    for t in range(1, tiles):
        edges = edges + got_ref[t]
    weight = jnp.maximum(add_edges(weight_ref[...], edges, 2, 2 * cap_rows), 1.0)
    for c in range(2):
        shifted = roll(acc[c * wide + map_lat : (c + 1) * wide], 1, 1)
        total = acc[c * wide : c * wide + map_lat] + jnp.where(lane_iota(shifted.shape) == 0, 0.0, shifted)
        out_ref[c] = add_edges(total, edges, c, 2 * cap_rows) / weight


def filter_constants(block_rows):
    az, rg, back, last = filter_tables(block_rows)
    az_h, az_l = host_split(az)
    rg_h, rg_l = host_split(rg)
    back_h, back_l = host_split(back)
    last_h, last_l = host_split(last)
    zero = np.zeros_like(back_l)
    lane = np.arange(LANES)
    same = lane[:, None] // PATCH == lane[None, :] // PATCH
    apart = (lane[:, None] - lane[None, :]) % PATCH
    near = (same & ((apart <= 1) | (apart == PATCH - 1))).astype(BF16)
    blocks = (
        np.concatenate([rg_h, rg_l], axis=0),
        np.concatenate([last_h, last_l], axis=0),
        np.concatenate([near, same.astype(BF16)], axis=1),
        np.concatenate([az_h, az_h, az_l], axis=1),
        np.concatenate([np.concatenate([back_h, back_h], axis=1), np.concatenate([back_l, zero], axis=1)], axis=0),
    )
    return np.concatenate([np.pad(b, ((0, 0), (0, 2 * LANES - b.shape[1]))) for b in blocks], axis=0)


def filter_scratch(rows, samples, block_rows, map_lat, map_lon, tiles):
    patches = samples // STEP
    count = block_rows * PATCH
    return (
        VMEM((6 * HALF, rows // HALF * (samples + LANES)), BF16),
        VMEM((patches // 2 * count, 2 * LANES), F32),
        VMEM((patches // 2 * count, 2 * LANES), BF16),
        VMEM((patches // 2 * count, LANES), F32),
        VMEM((patches // 2 * block_rows * 8, LANES), F32),
        VMEM((2 * count, patches * LANES), BF16),
        VMEM((2, map_lat, map_lon), F32),
        VMEM((16 * tiles, map_lat * map_lon), BF16),
        VMEM((16, map_lat, map_lon), F32),
    )


def swap_pairs(count, first):
    return [p for i in range(first, count - 1, 2) for p in ((i, i + 1), (i + 1, i))]


def scene(image, factor, heights, listing, position, owner, base, shares):
    n_az, n_rg = lax.axis_size("az"), lax.axis_size("rg")
    tiles = n_az * n_rg
    both = ("az", "rg")
    lats, lons, points = heights.shape
    slots = listing.shape[1]
    width = points // tiles
    packed = LANES // width
    lines, samples = factor.shape
    map_lat, map_lon = lines // LOOK, samples // LOOK
    block_rows = lines // STEP
    capacity = 2 * map_lat * map_lon // tiles
    cap_rows = -(-capacity // LANES)
    table_rows = -(-(3 * slots + cap_rows * packed) // packed)
    table_rows = -(-table_rows // 8) * 8
    early_rows = 4 * cap_rows
    late_rows = -(-(2 * cap_rows + 4) // 8) * 8
    slice_rows = lats * lons // packed
    parity = (lax.axis_index("az") % 2).astype(I32).reshape(1)
    rg = lax.axis_index("rg").astype(I32).reshape(1)

    def exchange(x):
        return lax.all_to_all(x, both, split_axis=0, concat_axis=0, tiled=True)

    slices = call(
        functools.partial(slice_kernel, width),
        sds((tiles, slice_rows + 8, LANES)),
        (heights, listing),
        grant=60,
    )
    got_slices = exchange(slices)
    one, two = call(halo_kernel, [sds((4, RIM, samples))] * 2, (parity, image, factor, position), smem=(0,))
    one = lax.ppermute(one, "az", swap_pairs(n_az, 0))
    two = lax.ppermute(two, "az", swap_pairs(n_az, 1))
    total = map_lat * map_lon
    looks_at = (owner.reshape(map_lat, map_lon), base.reshape(map_lat, map_lon), shares.reshape(4, map_lat, map_lon))
    early, cells, rim_sum, side_sum, at_m, at_n, *edges = call(
        functools.partial(pack_kernel, n_rg, cap_rows),
        [
            sds((tiles, early_rows, LANES)),
            sds((tiles, cap_rows * LANES)),
            sds((tiles, map_lon)),
            sds((tiles, map_lat)),
            sds((tiles, cap_rows * LANES), I32),
            sds((tiles, cap_rows * LANES), I32),
            sds((map_lon, total), BF16),
            sds((map_lat, total), BF16),
            sds((map_lat, total), BF16),
        ],
        looks_at,
        scratch=(VMEM((cap_rows * LANES, total), BF16), VMEM((3 * tiles, total), BF16), VMEM((8 * tiles, total), BF16), VMEM((8, map_lat, map_lon), F32)),
    )
    request = call(
        functools.partial(request_kernel, n_rg, (lats, lons), width, table_rows, slots),
        sds((tiles, table_rows + early_rows, LANES)),
        (got_slices, early, cells),
        scratch=(
            VMEM((packed, tiles * (slice_rows + 8), LANES), F32),
            VMEM((2, tiles, LANES), I32),
            pltpu.SMEM((2, tiles, LANES), I32),
            pltpu.SemaphoreType.DMA((1,)),
        ),
    )
    tables = exchange(request)
    flat, edge = call(
        functools.partial(flatten_kernel, width, table_rows, slots),
        [sds((2, lines + 2 * RIM, samples)), sds((2, lines + 2 * RIM, LANES))],
        (parity, tables, image, factor, position, one, two),
        smem=(0,),
        scratch=(
            VMEM((tiles // packed, packed * table_rows, LANES), F32),
            VMEM((3, lines + 2 * RIM, samples), F32),
            VMEM((lines + 2 * RIM, samples), I32),
        ),
    )
    edge = lax.ppermute(edge, "rg", swap_pairs(n_rg, 0))
    rows = lines + 2 * RIM
    packed_looks = call(
        functools.partial(filter_kernel, n_rg, cap_rows, block_rows),
        sds((tiles, late_rows, LANES)),
        (rg, flat, edge, rim_sum, side_sum, at_m, at_n, *looks_at, filter_constants(block_rows), *edges),
        smem=(0,),
        scratch=filter_scratch(rows, samples, block_rows, map_lat, map_lon, tiles),
    )
    got = exchange(packed_looks)
    wide = tiles * cap_rows * LANES
    hot, row_weights, weight_sum = call(
        functools.partial(prepare_kernel, cap_rows, table_rows, slots, width, map_lat),
        [sds((LANES, wide), BF16), sds((2 * map_lat, wide)), sds((map_lat, map_lon))],
        (tables,),
    )
    return call(
        functools.partial(splat_kernel, cap_rows, map_lat),
        sds((2, map_lat, map_lon)),
        (got, hot, row_weights, weight_sum),
        scratch=(VMEM((8 * map_lat, wide), BF16),),
    )


def solution(mesh):
    return jax.shard_map(
        scene,
        mesh=mesh,
        in_specs=(
            P(None, ("scene", "az"), "rg"),
            P(("scene", "az"), "rg"),
            P(("scene", "az"), "rg", None),
            P(("scene", "az", "rg"), None),
            P(("scene", "az"), "rg"),
            P(("scene", "az", "rg"), None),
            P(("scene", "az", "rg")),
            P(None, ("scene", "az", "rg")),
        ),
        out_specs=P(None, ("scene", "az"), "rg"),
        check_vma=False,
    )
```

```python
import functools
import math

import jax
import jax.numpy as jnp
import numpy as np
from jax import lax
from jax.experimental import pallas as pl
from jax.experimental.pallas import tpu as pltpu
from jax.sharding import PartitionSpec as P


PATCH = 64
LOOK = 4
EPS = 1e-06
LANES = 128
RIM = PATCH // 4
STEP = PATCH // 2
HALF = PATCH // 2
F32 = jnp.float32
BF16 = jnp.bfloat16
I32 = jnp.int32
VMEM = pltpu.VMEM
VSPEC = pl.BlockSpec(memory_space=pltpu.VMEM)
SSPEC = pl.BlockSpec(memory_space=pltpu.SMEM)


def call(kernel, outs, args, scratch=(), smem=(), grant=16, cost=(1_000_000, 1_000_000)):
    return pl.pallas_call(
        kernel,
        out_shape=outs,
        in_specs=[SSPEC if i in smem else VSPEC for i in range(len(args))],
        out_specs=jax.tree.map(lambda _: VSPEC, outs),
        scratch_shapes=list(scratch),
        compiler_params=pltpu.CompilerParams(vmem_limit_bytes=grant << 20),
        cost_estimate=pl.CostEstimate(flops=cost[0], bytes_accessed=cost[1], transcendentals=0),
    )(*args)


def sds(shape, dtype=F32):
    return jax.ShapeDtypeStruct(shape, dtype)


def split(x):
    hi = x.astype(BF16)
    return hi, (x - hi.astype(F32)).astype(BF16)


def dot(a, b):
    return jnp.dot(a, b, preferred_element_type=F32)


def dot_nt(a, b):
    return lax.dot_general(a, b, (((1,), (1,)), ((), ())), preferred_element_type=F32)


def fetch(pairs, sems):
    copies = [pltpu.make_async_copy(src, dst, sems.at[i]) for i, (src, dst) in enumerate(pairs)]
    for copy in copies:
        copy.start()
    return copies


def lane_iota(shape):
    return lax.broadcasted_iota(I32, shape, len(shape) - 1)


def row_iota(shape):
    return lax.broadcasted_iota(I32, shape, 0)


def roll(x, shift, axis):
    shift = shift % x.shape[axis]
    return x if shift == 0 else pltpu.roll(x, shift, axis)


def lane_gather(row, index):
    return jnp.take_along_axis(jnp.broadcast_to(row, index.shape), index, axis=1)


def host_split(x):
    hi = np.asarray(x, np.float32).astype(BF16)
    lo = (np.asarray(x, np.float64) - hi.astype(np.float64)).astype(BF16)
    return hi, lo


def filter_tables(block_rows):
    turn = 2.0 * math.pi / PATCH
    step = np.arange(PATCH)
    cosine = np.cos(turn * (step[:, None] * step[None, :] % PATCH))
    sine = np.sin(turn * (step[:, None] * step[None, :] % PATCH))
    count = block_rows * PATCH
    az = np.zeros((2 * PATCH, 2 * HALF))
    az[:PATCH, :HALF], az[:PATCH, HALF:] = cosine[:, :HALF], sine[:, :HALF]
    az[PATCH:, :HALF], az[PATCH:, HALF:] = -sine[:, :HALF], cosine[:, :HALF]
    rg = np.zeros((2 * LANES, 4 * PATCH))
    for p in range(2):
        w, wi = slice(p * HALF, p * HALF + PATCH), slice(LANES + p * HALF, LANES + p * HALF + PATCH)
        lr, li = slice(p * PATCH, (p + 1) * PATCH), slice(LANES + p * PATCH, LANES + (p + 1) * PATCH)
        rg[w, lr], rg[wi, lr] = cosine, sine
        rg[w, li], rg[wi, li] = -sine, cosine
    looks = STEP // LOOK
    core = cosine[RIM : RIM + STEP].reshape(looks, LOOK, PATCH).mean(axis=1)
    core_s = sine[RIM : RIM + STEP].reshape(looks, LOOK, PATCH).mean(axis=1)
    back = np.zeros((2 * block_rows * looks, count))
    for u in range(block_rows):
        k = slice(u * PATCH, (u + 1) * PATCH)
        back[u * looks : (u + 1) * looks, k] = core / PATCH
        back[(block_rows + u) * looks : (block_rows + u + 1) * looks, k] = core_s / PATCH
    c_l, s_l = core.T / PATCH, core_s.T / PATCH
    reps = LANES // looks
    patch_of = np.arange(LANES) // looks % 2
    last = np.zeros((4 * LANES, 2 * LANES))
    terms = ((c_l, s_l), (-s_l, c_l), (-s_l, c_l), (-c_l, -s_l))
    for i, (re, im) in enumerate(terms):
        for p in range(2):
            k = slice(i * LANES + p * PATCH, i * LANES + (p + 1) * PATCH)
            last[k, :LANES] = np.tile(re, reps) * (patch_of == p)
            last[k, LANES:] = np.tile(im, reps) * (patch_of == p)
    return az, rg, back, last


def slice_kernel(width, dem_ref, list_ref, out_ref):
    tiles = out_ref.shape[0]
    lats, lons, _ = dem_ref.shape
    packed = LANES // width
    groups = lats // packed
    slots = list_ref.shape[1]
    lane = lane_iota((lons, LANES))
    listed = list_ref[...].astype(F32)
    for q in range(tiles):
        tile, offset = divmod(q * width, LANES)
        for g in range(groups):
            total = None
            for p in range(packed):
                x = dem_ref[p * groups + g, :, tile * LANES : (tile + 1) * LANES]
                x = roll(x, p * width - offset, 1)
                total = x if total is None else jnp.where(lane // width == p, x, total)
            out_ref[q, g * lons : (g + 1) * lons, :] = total
        out_ref[q, groups * lons : groups * lons + 1, 0:slots] = listed


def halo_kernel(par_ref, image_ref, factor_ref, position_ref, one_ref, two_ref):
    even = par_ref[0] == 0
    lines = factor_ref.shape[0]
    fields = (
        lambda s: image_ref[0, s, :],
        lambda s: image_ref[1, s, :],
        lambda s: factor_ref[s, :],
        lambda s: position_ref[s, :].astype(F32),
    )
    for i, field in enumerate(fields):
        first = field(slice(0, RIM))
        last = field(slice(lines - RIM, lines))
        one_ref[i] = jnp.where(even, last, first)
        two_ref[i] = jnp.where(even, first, last)


def border_sums(n_rg, tiles, values, owner_ref, base_ref, share_ref, w_ref, term_ref, col_ref, here_ref, next_ref):
    channels = len(values)
    height, width = owner_ref.shape
    base = base_ref[...]
    last_line = jnp.right_shift(base, width.bit_length() - 1) == height - 1
    last_column = jnp.bitwise_and(base, width - 1) == width - 1
    owner = owner_ref[...]
    on_line = jnp.where(last_line, owner, -1)
    on_column = jnp.where(last_column, owner, -1)
    terms = []
    for c, value in enumerate(values):
        for i in range(2):
            spot = (i * channels + c) * tiles
            far = 4 * channels * tiles + spot
            for mask, k, row in ((0, 2, 2 * spot), (0, 3, 2 * spot + tiles), (1, 1, far), (1, 3, far + 2 * channels * tiles)):
                x = share_ref[k] if value is None else share_ref[k] * value
                high = x.astype(BF16).astype(F32)
                term_ref[len(terms)] = high if i == 0 else x - high
                terms.append((mask, row))
    tile = row_iota((tiles, width))
    for m in range(height):
        cut = slice(m * width, (m + 1) * width)
        masks = (tile == on_line[m : m + 1], tile == on_column[m : m + 1])
        for n, (mask, row) in enumerate(terms):
            w_ref[row : row + tiles, cut] = jnp.where(masks[mask], term_ref[n, m : m + 1, :], 0.0).astype(BF16)
    size = channels * tiles
    b = dot_nt(w_ref[0 : 4 * size], col_ref[...])
    b = b[: 2 * size] + b[2 * size :]
    side = dot_nt(w_ref[4 * size : 6 * size], here_ref[...]) + dot_nt(w_ref[6 * size : 8 * size], next_ref[...])
    side = side[:size] + side[size:]
    results = []
    for c in range(channels):
        b0, b1 = b[2 * c * tiles : (2 * c + 1) * tiles], b[(2 * c + 1) * tiles : (2 * c + 2) * tiles]
        dest = row_iota(b0.shape)
        shifted = roll(b1, 1, 1)
        below = roll(b0, n_rg, 0)
        beside = roll(shifted, n_rg, 0)
        diagonal = jnp.where(dest % n_rg > 0, roll(shifted, n_rg + 1, 0), 0.0)
        beside = jnp.where(lane_iota(b0.shape) == 0, diagonal, beside)
        rows = jnp.where(dest >= n_rg, below + beside, 0.0)
        one = side[c * tiles : (c + 1) * tiles]
        one = jnp.concatenate([jnp.zeros((1, one.shape[1]), F32), one[:-1]], axis=0)
        results.append((rows, jnp.where(row_iota(one.shape) % n_rg > 0, one, 0.0)))
    return results


def add_edges(total, edges, channel, first):
    rows, lanes = row_iota(total.shape), lane_iota(total.shape)
    edge, side = edges[first + channel : first + channel + 1], edges[first + 3 : first + 4]
    column = jnp.sum(jnp.where(lanes == rows + channel * total.shape[0], side, 0.0), axis=1, keepdims=True)
    return total + jnp.where(rows == 0, edge, 0.0) + jnp.where(lanes == 0, column, 0.0)


def pack_kernel(n_rg, cap_rows, owner_ref, base_ref, share_ref, early_ref, cell_ref, rim_ref, side_ref, im_ref, in_ref, col_ref, here_ref, next_ref, hot_ref, lhs_ref, w_ref, term_ref):
    tiles = early_ref.shape[0]
    height, width = owner_ref.shape
    owner = owner_ref[...]
    batch = min(tiles, 16)
    tri = (row_iota((width, width)) < lane_iota((width, width))).astype(BF16)
    ones = jnp.ones((width, width), BF16)
    size = batch * height
    r, c = row_iota((size, size)), lane_iota((size, size))
    lower = ((r // height == c // height) & (c < r)).astype(BF16)
    rank = jnp.zeros((height, width), F32)
    for b in range(tiles // batch):
        hot = jnp.concatenate([(owner == b * batch + o).astype(F32) for o in range(batch)], axis=0)
        hot16 = hot.astype(BF16)
        before = dot(hot16, tri) + dot(lower, dot(hot16, ones).astype(BF16))
        kept = hot * before
        for o in range(batch):
            rank = rank + kept[o * height : (o + 1) * height]
    rank = rank.astype(I32)
    base = base_ref[...]
    shift = width.bit_length() - 1
    column = jnp.bitwise_and(base, width - 1)
    line = jnp.right_shift(base, shift)
    cap = cap_rows * LANES
    for m in range(height):
        cut = slice(m * width, (m + 1) * width)
        hot_ref[:, cut] = (row_iota((cap, width)) == rank[m : m + 1]).astype(F32).astype(BF16)
        col_ref[:, cut] = (row_iota((width, width)) == column[m : m + 1]).astype(F32).astype(BF16)
        mine = row_iota((tiles, width)) == owner[m : m + 1]
        lhs_ref[0:tiles, cut] = mine.astype(F32).astype(BF16)
        lhs_ref[tiles : 2 * tiles, cut] = jnp.where(mine, float(m), 0.0).astype(BF16)
        lhs_ref[2 * tiles :, cut] = jnp.where(mine, lane_iota((tiles, width)).astype(F32), 0.0).astype(BF16)
        at = row_iota((height, width))
        here_ref[:, cut] = (at == line[m : m + 1]).astype(F32).astype(BF16)
        next_ref[:, cut] = (at == line[m : m + 1] + 1).astype(F32).astype(BF16)
    found = dot_nt(lhs_ref[...], hot_ref[...])
    valid = found[0:tiles] > 0.5
    at_m = found[tiles : 2 * tiles].astype(I32)
    at_n = found[2 * tiles :].astype(I32)
    im_ref[...] = at_m
    in_ref[...] = at_n
    cell = base.astype(F32)
    for channel in range(5):
        for k in range(cap_rows):
            cut = slice(k * LANES, (k + 1) * LANES)
            total = jnp.zeros((tiles, LANES), F32)
            for m in range(height):
                row = cell[m : m + 1] if channel == 4 else share_ref[channel, m : m + 1, :]
                total = jnp.where(at_m[:, cut] == m, lane_gather(row, at_n[:, cut]), total)
            total = jnp.where(valid[:, cut], total, 0.0)
            if channel == 4:
                cell_ref[:, cut] = total
            else:
                early_ref[:, channel * cap_rows + k, :] = total
    ((rows, side),) = border_sums(n_rg, tiles, [None], owner_ref, base_ref, share_ref, w_ref, term_ref, col_ref, here_ref, next_ref)
    rim_ref[...] = rows
    side_ref[...] = side


def request_kernel(n_rg, grid, width, table_rows, slots, got_ref, early_ref, cell_ref, out_ref, turn_ref, list_ref, index_ref, sem):
    tiles, rows, _ = got_ref.shape
    lats, lons = grid
    packed = LANES // width
    groups = lats // packed
    listed = jnp.maximum(got_ref[:, rows - 8, :], 0.0)
    listed = jnp.where(lane_iota(listed.shape) < slots, listed, 0.0).astype(I32)
    lat, lon = listed // (lons * n_rg), listed % (lons * n_rg)
    key = lat // lats * n_rg + lon // lons
    row, piece = key * rows + lat % lats % groups * lons + lon % lons, lat % lats // groups
    for place in range(packed):
        list_ref[place] = jnp.bitwise_and(place - piece, packed - 1) * (tiles * rows) + row
    (copy,) = fetch(((list_ref, index_ref),), sem)
    for t in range(tiles):
        x = got_ref[t]
        for p in range(packed):
            at = (p * tiles + t) * rows
            turn_ref[at : at + rows, :] = roll(x, p * width, 1)
        out_ref[t, table_rows:, :] = early_ref[t]
    for k in range(cell_ref.shape[1] // LANES):
        x = cell_ref[:, k * LANES : (k + 1) * LANES]
        for i in range(packed):
            place, line = divmod(3 * slots + k * packed + i, table_rows)
            cut = slice(place * width, (place + 1) * width)
            out_ref[:, line, cut] = roll(x, (place - i) * width, 1)[:, cut]
    copy.wait()
    for t in range(tiles):
        for f in range(slots):
            found = {}
            for n, dest in ((0, t + n_rg), (1, t), (2, t - n_rg)):
                if 0 <= dest < tiles:
                    place, line = divmod(n * slots + f, table_rows)
                    if place not in found:
                        found[place] = turn_ref[pl.ds(index_ref[place, t, f], 1), :]
                    cut = slice(place * width, (place + 1) * width)
                    out_ref[dest, line : line + 1, cut] = found[place][:, cut]


def sincos(x):
    n = jnp.floor(x * (2.0 / math.pi) + 0.5)
    r = x - n * 1.5703125
    r = r - n * 4.837512969970703e-4
    r = r - n * 7.549789954891882e-8
    z = r * r
    s = ((-1.9515295891e-4 * z + 8.3321608736e-3) * z - 1.6666654611e-1) * z * r + r
    c = ((2.443315711809948e-5 * z - 1.388731625493765e-3) * z + 4.166664568298827e-2) * z * z - 0.5 * z + 1.0
    q = n.astype(I32)
    odd = (q & 1) == 1
    sine = jnp.where(odd, c, s)
    cosine = jnp.where(odd, s, c)
    sine = jnp.where((q & 2) == 2, -sine, sine)
    cosine = jnp.where(((q + 1) & 2) == 2, -cosine, cosine)
    return cosine, sine


def flatten_kernel(width, table_rows, slots, par_ref, got_ref, image_ref, factor_ref, position_ref, one_ref, two_ref, flat_ref, edge_ref, tab_ref):
    even = par_ref[0] == 0
    lines, samples = factor_ref.shape
    packed = LANES // width
    tiles = got_ref.shape[0]
    parts = tiles // packed
    lane = lane_iota((table_rows, LANES))
    for k in range(parts):
        for place in range(packed):
            total = None
            for j in range(packed):
                x = roll(got_ref[k * packed + j, 0:table_rows, :], (j - place) * width, 1)
                total = x if total is None else jnp.where(lane // width == j, x, total)
            tab_ref[k, place * table_rows : (place + 1) * table_rows, :] = total
    cols = samples // LANES
    shift = LANES.bit_length() - 1
    part_bits = parts.bit_length() - 1
    own = (lambda c: (lambda spot: image_ref[(c, *spot)]))

    def rim_field(n, below):
        def read(spot):
            a, b = one_ref[(n, *spot)], two_ref[(n, *spot)]
            return jnp.where(even, a, b) if below else jnp.where(even, b, a)

        return read

    fields = [own(0), own(1), lambda spot: factor_ref[spot], lambda spot: position_ref[spot]]
    strips = [(0, [rim_field(n, False) for n in range(4)], RIM), (1, fields, lines), (2, [rim_field(n, True) for n in range(4)], RIM)]
    line = 0
    for table, sources, height in strips:
        for start in range(0, height, 8):
            for c in range(cols):
                spot = (slice(start, start + 8), slice(c * LANES, (c + 1) * LANES))
                re, im, factor, at = [read(spot) for read in sources]
                at = at.astype(I32)
                lanes = jnp.bitwise_and(at, LANES - 1)
                bits = [jnp.bitwise_and(at, LANES << b) != 0 for b in range(part_bits)]
                slot = jnp.right_shift(at, shift + part_bits)
                found = None
                for f in range(slots):
                    row = table * slots + f
                    x = [
                        jnp.take_along_axis(jnp.broadcast_to(tab_ref[k, row : row + 1, :], (8, LANES)), lanes, axis=1)
                        for k in range(parts)
                    ]
                    for bit in bits:
                        x = [jnp.where(bit, x[n + 1], x[n]) for n in range(0, len(x), 2)]
                    found = x[0] if f == 0 else jnp.where(slot == f, x[0], found)
                cosine, sine = sincos(factor * found)
                flat_ref[0, line : line + 8, spot[1]] = re * cosine + im * sine
                flat_ref[1, line : line + 8, spot[1]] = im * cosine - re * sine
            line += 8
    edge = lane_iota((lines + 2 * RIM, LANES))
    for c in range(2):
        first = flat_ref[c, :, 0:LANES]
        last = roll(flat_ref[c, :, samples - LANES : samples], 2 * RIM, 1)
        edge_ref[c] = jnp.where(edge < RIM, first, jnp.where(edge < 2 * RIM, last, 0.0))


def root(x):
    return x * lax.rsqrt(jnp.maximum(x, 1e-37))


def stack_parts(x_ref, c, at, x):
    high, low = split(x)
    x_ref[c * HALF : (c + 1) * HALF, at] = high
    x_ref[(2 + c) * HALF : (3 + c) * HALF, at] = low
    x_ref[(4 + c) * HALF : (5 + c) * HALF, at] = high


def spectrum(strips):
    flip = jnp.where(row_iota(strips[0].shape) % 2 == 0, 1.0, -1.0)
    return jnp.concatenate([one + flip * two for one, two in zip(strips[:-1], strips[1:])], axis=0)


def range_dft(windows, const_ref):
    (rh, rl), (ih, il) = [split(jnp.concatenate(x, axis=0)) for x in windows]
    size = 2 * LANES
    main, rest = const_ref[:size], const_ref[size : 2 * size]
    return dot(jnp.concatenate([rh, ih, rl, il, rh, ih], axis=1), jnp.concatenate([main, main, rest], axis=0))


def transform_kernel(flat_ref, az_ref, const_ref, out_ref, x_ref):
    _, rows, samples = flat_ref.shape
    cols = samples // LANES
    wide = (cols + 1) * LANES
    lane = lane_iota((HALF, LANES))
    for p in range(rows // HALF):
        for c in range(2):
            before = 0.0
            for j in range(cols + 1):
                now = 0.0
                if j < cols:
                    now = roll(flat_ref[c, p * HALF : (p + 1) * HALF, j * LANES : (j + 1) * LANES], RIM, 1)
                at = slice(p * wide + j * LANES, p * wide + (j + 1) * LANES)
                stack_parts(x_ref, c, at, jnp.where(lane < RIM, before, now))
                before = now
    e = dot(az_ref[...], x_ref[...])
    windows = []
    for c in range(2):
        cut = slice(c * PATCH, (c + 1) * PATCH)
        cells = [
            spectrum([e[cut, p * wide + j * LANES : p * wide + (j + 1) * LANES] for p in range(rows // HALF)])
            for j in range(cols + 1)
        ]
        half = lane_iota(cells[0].shape) < PATCH
        turned = [pltpu.roll(x, PATCH, 1) for x in cells]
        found = []
        for j in range(cols):
            found += [cells[j], jnp.where(half, turned[j], turned[j + 1])]
        windows.append(found)
    out_ref[...] = range_dft(windows, const_ref)


def filter_kernel(n_rg, cap_rows, block_rows, rg_ref, y_ref, edge_ref, rim_ref, side_ref, im_ref, in_ref, owner_ref, base_ref, share_ref, az_ref, const_ref, col_ref, here_ref, next_ref, out_ref, x_ref, rim_y_ref, m_ref, s_ref, p_ref, z_ref, look_ref, w_ref, term_ref):
    strips = edge_ref.shape[1] // HALF
    lane = lane_iota((HALF, LANES))
    left = rg_ref[0] > 0
    right = rg_ref[0] < n_rg - 1
    for p in range(strips):
        for c in range(2):
            halo = edge_ref[c, p * HALF : (p + 1) * HALF]
            before = jnp.where(left, roll(halo, -RIM, 1), 0.0)
            after = jnp.where(right & (lane < 2 * RIM), roll(halo, RIM, 1), 0.0)
            stack_parts(x_ref, c, slice(p * LANES, (p + 1) * LANES), jnp.where(lane < RIM, before, after))
    looks = block_rows * STEP // LOOK
    block = const_ref[...]

    def tripled(at, size):
        return jnp.concatenate([block[at : at + size], block[at : at + size], block[at + size : at + 2 * size]], axis=0)

    last3 = tripled(4 * LANES, 4 * LANES)
    near = jnp.concatenate([block[12 * LANES : 13 * LANES, :LANES]] * 2, axis=0)
    side = jnp.concatenate([block[12 * LANES : 13 * LANES, LANES:]] * 2, axis=0)
    back = block[13 * LANES : 13 * LANES + 4 * looks, : 2 * block_rows * PATCH]
    rim = dot(az_ref[...], x_ref[...])
    count = block_rows * PATCH
    pairs = y_ref.shape[0] // count
    windows = []
    for c in range(2):
        x = spectrum([rim[c * PATCH : (c + 1) * PATCH, p * LANES : (p + 1) * LANES] for p in range(strips)])
        first = lane_iota(x.shape) < RIM
        windows.append([jnp.where(first, x, 0.0), pltpu.roll(jnp.where(first, 0.0, x), PATCH, 1)])
    rim_y_ref[...] = range_dft(windows, const_ref)
    rim_y_ref[:count] = rim_y_ref[:count] + y_ref[:count]
    rim_y_ref[count:] = rim_y_ref[count:] + y_ref[(pairs - 1) * count :]

    def everywhere(step):
        step(0, rim_y_ref, 0)
        pl.loop(1, pairs - 1, unroll=3)(lambda w: step(w, y_ref, w))
        step(pairs - 1, rim_y_ref, 1)

    def measure(w, ref, place):
        at = pl.multiple_of(w * count, count)
        cut = pl.ds(pl.multiple_of(place * count, count), count)
        re, im = ref[cut, :LANES], ref[cut, LANES:]
        magnitude = root(re * re + im * im)
        high, low = split(magnitude)
        m_ref[pl.ds(at, count), :LANES] = high
        m_ref[pl.ds(at, count), LANES:] = low
        for u in range(block_rows):
            part = magnitude[u * PATCH : u * PATCH + 8]
            for i in range(1, PATCH // 8):
                part = part + magnitude[u * PATCH + 8 * i : u * PATCH + 8 * i + 8]
            p_ref[pl.ds(pl.multiple_of((w * block_rows + u) * 8, 8), 8), :] = part

    everywhere(measure)
    s_ref[...] = dot(m_ref[...], near)
    ph, plow = split(p_ref[...])
    sums = dot(jnp.concatenate([ph, plow], axis=1), side)
    for n in range(pairs * block_rows):
        x = sums[8 * n : 8 * n + 8]
        for shift in (4, 2, 1):
            x = x + pltpu.roll(x, shift, 0)
        p_ref[8 * n : 8 * n + 8, :] = 1.0 / (9.0 * (x * (1.0 / (PATCH * PATCH)) + EPS))

    def weigh(w, ref, place):
        at = pl.multiple_of(w * 2 * LANES, 2 * LANES)
        for u in range(block_rows):
            cut = pl.ds(pl.multiple_of(w * count + u * PATCH, PATCH), PATCH)
            su = s_ref[cut, :]
            su = su + pltpu.roll(su, 1, 0) + pltpu.roll(su, PATCH - 1, 0)
            factor = p_ref[pl.ds(pl.multiple_of((w * block_rows + u) * 8, 8), 8), :]
            gain = root(su * jnp.concatenate([factor] * (PATCH // 8), axis=0))
            for c in range(2):
                source = pl.ds(pl.multiple_of(place * count + u * PATCH, PATCH), PATCH)
                high, low = split(ref[source, c * LANES : (c + 1) * LANES] * gain)
                span = pl.ds(pl.multiple_of(at + c * LANES, LANES), LANES)
                z_ref[u * PATCH : (u + 1) * PATCH, span] = high
                z_ref[count + u * PATCH : count + (u + 1) * PATCH, span] = low

    everywhere(weigh)
    t = dot(back, z_ref[...])
    t = t[: 2 * looks] + t[2 * looks :]
    stacked = jnp.concatenate(
        [
            jnp.concatenate([t[i * looks : (i + 1) * looks, w * 2 * LANES : (w + 1) * 2 * LANES] for i in range(2)], axis=1)
            for w in range(pairs)
        ],
        axis=0,
    )
    sh, sl = split(stacked)
    y = dot(jnp.concatenate([sh, sl, sh], axis=1), last3)
    group = lane_iota((looks, LANES)) // (2 * STEP // LOOK)
    for c in range(2):
        total = jnp.zeros((looks, LANES), F32)
        for w in range(pairs):
            total = jnp.where(group == w, y[w * looks : (w + 1) * looks, c * LANES : (c + 1) * LANES], total)
        look_ref[c] = total
    tiles = out_ref.shape[0]
    for k in range(cap_rows):
        cut = slice(k * LANES, (k + 1) * LANES)
        at_m, at_n = im_ref[:, cut], in_ref[:, cut]
        for c in range(2):
            total = jnp.zeros((tiles, LANES), F32)
            for m in range(looks):
                total = jnp.where(at_m == m, lane_gather(look_ref[c, m : m + 1, :], at_n), total)
            out_ref[:, c * cap_rows + k, :] = total
    values = [look_ref[0], look_ref[1]]
    borders = border_sums(n_rg, tiles, values, owner_ref, base_ref, share_ref, w_ref, term_ref, col_ref, here_ref, next_ref)
    for c, (rows, side) in enumerate(borders):
        out_ref[:, 2 * cap_rows + c, :] = rows
        out_ref[:, 2 * cap_rows + 3, c * looks : (c + 1) * looks] = side
    out_ref[:, 2 * cap_rows + 2, :] = rim_ref[...]
    out_ref[:, 2 * cap_rows + 3, 2 * looks : 3 * looks] = side_ref[...]


def prepare_kernel(cap_rows, table_rows, slots, width, map_lat, got_ref, hot_ref, row_ref, sum_ref):
    tiles = got_ref.shape[0]
    packed = LANES // width
    lane = lane_iota((1, LANES))
    for t in range(tiles):
        for k in range(cap_rows):
            def channel(c):
                return got_ref[t, table_rows + c * cap_rows + k : table_rows + c * cap_rows + k + 1, :]

            cell = None
            for i in range(packed):
                place, spot = divmod(3 * slots + k * packed + i, table_rows)
                x = roll(got_ref[t, spot : spot + 1, :], (i - place) * width, 1)
                cell = x if cell is None else jnp.where(lane // width == i, x, cell)
            cell = cell.astype(I32)
            line, column = jnp.right_shift(cell, LANES.bit_length() - 1), jnp.bitwise_and(cell, LANES - 1)
            at = (t * cap_rows + k) * LANES
            cut = slice(at, at + LANES)
            hot_ref[:, cut] = (row_iota((LANES, LANES)) == column).astype(F32).astype(BF16)
            rows = row_iota((map_lat, LANES))
            here, next_line = rows == line, rows == line + 1
            for d in range(2):
                row_ref[d * map_lat : (d + 1) * map_lat, cut] = jnp.where(here, channel(d), 0.0) + jnp.where(
                    next_line, channel(2 + d), 0.0
                )
    high, low = split(row_ref[...])
    acc = dot_nt(high, hot_ref[...]) + dot_nt(low, hot_ref[...])
    shifted = roll(acc[map_lat:], 1, 1)
    total = acc[:map_lat] + jnp.where(lane_iota(shifted.shape) == 0, 0.0, shifted)
    sum_ref[...] = total


def splat_kernel(cap_rows, map_lat, got_ref, hot_ref, row_ref, weight_ref, out_ref, x_ref):
    tiles = got_ref.shape[0]
    wide = 2 * map_lat
    for t in range(tiles):
        for k in range(cap_rows):
            cut = slice((t * cap_rows + k) * LANES, (t * cap_rows + k + 1) * LANES)
            for c in range(2):
                value = got_ref[t, c * cap_rows + k : c * cap_rows + k + 1, :]
                high, low = split(row_ref[:, cut] * value)
                x_ref[c * wide : (c + 1) * wide, cut] = high
                x_ref[(2 + c) * wide : (3 + c) * wide, cut] = low
    acc = dot_nt(x_ref[...], hot_ref[...])
    acc = acc[: 2 * wide] + acc[2 * wide :]
    edges = got_ref[0]
    for t in range(1, tiles):
        edges = edges + got_ref[t]
    weight = jnp.maximum(add_edges(weight_ref[...], edges, 2, 2 * cap_rows), 1.0)
    for c in range(2):
        shifted = roll(acc[c * wide + map_lat : (c + 1) * wide], 1, 1)
        total = acc[c * wide : c * wide + map_lat] + jnp.where(lane_iota(shifted.shape) == 0, 0.0, shifted)
        out_ref[c] = add_edges(total, edges, c, 2 * cap_rows) / weight


def filter_constants(block_rows):
    az, rg, back, last = filter_tables(block_rows)
    az_h, az_l = host_split(az)
    rg_h, rg_l = host_split(rg)
    back_h, back_l = host_split(back)
    last_h, last_l = host_split(last)
    zero = np.zeros_like(back_l)
    lane = np.arange(LANES)
    same = lane[:, None] // PATCH == lane[None, :] // PATCH
    apart = (lane[:, None] - lane[None, :]) % PATCH
    near = (same & ((apart <= 1) | (apart == PATCH - 1))).astype(BF16)
    blocks = (
        np.concatenate([rg_h, rg_l], axis=0),
        np.concatenate([last_h, last_l], axis=0),
        np.concatenate([near, same.astype(BF16)], axis=1),
        np.concatenate([np.concatenate([back_h, back_h], axis=1), np.concatenate([back_l, zero], axis=1)], axis=0),
    )
    wide = [np.pad(b, ((0, 0), (0, 2 * LANES - b.shape[1]))) for b in blocks]
    return np.concatenate([az_h, az_h, az_l], axis=1), np.concatenate(wide, axis=0)


def filter_scratch(rows, samples, block_rows, map_lat, map_lon, tiles):
    patches = samples // STEP
    count = block_rows * PATCH
    return (
        VMEM((6 * HALF, rows // HALF * LANES), BF16),
        VMEM((2 * count, 2 * LANES), F32),
        VMEM((patches // 2 * count, 2 * LANES), BF16),
        VMEM((patches // 2 * count, LANES), F32),
        VMEM((patches // 2 * block_rows * 8, LANES), F32),
        VMEM((2 * count, patches * LANES), BF16),
        VMEM((2, map_lat, map_lon), F32),
        VMEM((16 * tiles, map_lat * map_lon), BF16),
        VMEM((16, map_lat, map_lon), F32),
    )


def swap_pairs(count, first):
    return [p for i in range(first, count - 1, 2) for p in ((i, i + 1), (i + 1, i))]


def scene(image, factor, heights, listing, position, owner, base, shares):
    n_az, n_rg = lax.axis_size("az"), lax.axis_size("rg")
    tiles = n_az * n_rg
    both = ("az", "rg")
    lats, lons, points = heights.shape
    slots = listing.shape[1]
    width = points // tiles
    packed = LANES // width
    lines, samples = factor.shape
    map_lat, map_lon = lines // LOOK, samples // LOOK
    block_rows = lines // STEP
    capacity = 2 * map_lat * map_lon // tiles
    cap_rows = -(-capacity // LANES)
    table_rows = -(-(3 * slots + cap_rows * packed) // packed)
    table_rows = -(-table_rows // 8) * 8
    early_rows = 4 * cap_rows
    late_rows = -(-(2 * cap_rows + 4) // 8) * 8
    slice_rows = lats * lons // packed
    parity = (lax.axis_index("az") % 2).astype(I32).reshape(1)
    rg = lax.axis_index("rg").astype(I32).reshape(1)

    def exchange(x):
        return lax.all_to_all(x, both, split_axis=0, concat_axis=0, tiled=True)

    slices = call(
        functools.partial(slice_kernel, width),
        sds((tiles, slice_rows + 8, LANES)),
        (heights, listing),
        grant=60,
    )
    got_slices = exchange(slices)
    one, two = call(halo_kernel, [sds((4, RIM, samples))] * 2, (parity, image, factor, position), smem=(0,))
    one = lax.ppermute(one, "az", swap_pairs(n_az, 0))
    two = lax.ppermute(two, "az", swap_pairs(n_az, 1))
    total = map_lat * map_lon
    looks_at = (owner.reshape(map_lat, map_lon), base.reshape(map_lat, map_lon), shares.reshape(4, map_lat, map_lon))
    early, cells, rim_sum, side_sum, at_m, at_n, *edges = call(
        functools.partial(pack_kernel, n_rg, cap_rows),
        [
            sds((tiles, early_rows, LANES)),
            sds((tiles, cap_rows * LANES)),
            sds((tiles, map_lon)),
            sds((tiles, map_lat)),
            sds((tiles, cap_rows * LANES), I32),
            sds((tiles, cap_rows * LANES), I32),
            sds((map_lon, total), BF16),
            sds((map_lat, total), BF16),
            sds((map_lat, total), BF16),
        ],
        looks_at,
        scratch=(VMEM((cap_rows * LANES, total), BF16), VMEM((3 * tiles, total), BF16), VMEM((8 * tiles, total), BF16), VMEM((8, map_lat, map_lon), F32)),
    )
    request = call(
        functools.partial(request_kernel, n_rg, (lats, lons), width, table_rows, slots),
        sds((tiles, table_rows + early_rows, LANES)),
        (got_slices, early, cells),
        scratch=(
            VMEM((packed * tiles * (slice_rows + 8), LANES), F32),
            VMEM((packed, tiles, LANES), I32),
            pltpu.SMEM((packed, tiles, LANES), I32),
            pltpu.SemaphoreType.DMA((1,)),
        ),
    )
    tables = exchange(request)
    flat, edge = call(
        functools.partial(flatten_kernel, width, table_rows, slots),
        [sds((2, lines + 2 * RIM, samples)), sds((2, lines + 2 * RIM, LANES))],
        (parity, tables, image, factor, position, one, two),
        smem=(0,),
        scratch=(
            VMEM((tiles // packed, packed * table_rows, LANES), F32),
        ),
    )
    edge = lax.ppermute(edge, "rg", swap_pairs(n_rg, 0))
    az_parts, constants = filter_constants(block_rows)
    wide = (lines + 2 * RIM) // HALF * (samples + LANES)
    patches = samples // STEP
    count = block_rows * PATCH
    lines_done = call(
        transform_kernel,
        sds((patches // 2 * count, 2 * LANES)),
        (flat, az_parts, constants),
        scratch=(VMEM((6 * HALF, wide), BF16),),
    )
    rows = lines + 2 * RIM
    patches = samples // STEP
    count = block_rows * PATCH
    packed_looks = call(
        functools.partial(filter_kernel, n_rg, cap_rows, block_rows),
        sds((tiles, late_rows, LANES)),
        (rg, lines_done, edge, rim_sum, side_sum, at_m, at_n, *looks_at, az_parts, constants, *edges),
        smem=(0,),
        scratch=filter_scratch(rows, samples, block_rows, map_lat, map_lon, tiles),
    )
    got = exchange(packed_looks)
    wide = tiles * cap_rows * LANES
    hot, row_weights, weight_sum = call(
        functools.partial(prepare_kernel, cap_rows, table_rows, slots, width, map_lat),
        [sds((LANES, wide), BF16), sds((2 * map_lat, wide)), sds((map_lat, map_lon))],
        (tables,),
    )
    return call(
        functools.partial(splat_kernel, cap_rows, map_lat),
        sds((2, map_lat, map_lon)),
        (got, hot, row_weights, weight_sum),
        scratch=(VMEM((8 * map_lat, wide), BF16),),
    )


def solution(mesh):
    return jax.shard_map(
        scene,
        mesh=mesh,
        in_specs=(
            P(None, ("scene", "az"), "rg"),
            P(("scene", "az"), "rg"),
            P(("scene", "az"), "rg", None),
            P(("scene", "az", "rg"), None),
            P(("scene", "az"), "rg"),
            P(("scene", "az", "rg"), None),
            P(("scene", "az", "rg")),
            P(None, ("scene", "az", "rg")),
        ),
        out_specs=P(None, ("scene", "az"), "rg"),
        check_vma=False,
    )
```

```python
import functools
import math

import jax
import jax.numpy as jnp
import numpy as np
from jax import lax
from jax.experimental import pallas as pl
from jax.experimental.pallas import tpu as pltpu
from jax.sharding import PartitionSpec as P


PATCH = 64
LOOK = 4
EPS = 1e-06
LANES = 128
QUAD = 1
RIM = PATCH // 4
STEP = PATCH // 2
HALF = PATCH // 2
F32 = jnp.float32
BF16 = jnp.bfloat16
I32 = jnp.int32
VMEM = pltpu.VMEM
VSPEC = pl.BlockSpec(memory_space=pltpu.VMEM)
SSPEC = pl.BlockSpec(memory_space=pltpu.SMEM)


def call(kernel, outs, args, scratch=(), smem=(), grant=16, cost=(1_000_000, 1_000_000)):
    return pl.pallas_call(
        kernel,
        out_shape=outs,
        in_specs=[SSPEC if i in smem else VSPEC for i in range(len(args))],
        out_specs=jax.tree.map(lambda _: VSPEC, outs),
        scratch_shapes=list(scratch),
        compiler_params=pltpu.CompilerParams(vmem_limit_bytes=grant << 20),
        cost_estimate=pl.CostEstimate(flops=cost[0], bytes_accessed=cost[1], transcendentals=0),
    )(*args)


def sds(shape, dtype=F32):
    return jax.ShapeDtypeStruct(shape, dtype)


def split(x):
    hi = x.astype(BF16)
    return hi, (x - hi.astype(F32)).astype(BF16)


def dot(a, b):
    return jnp.dot(a, b, preferred_element_type=F32)


def dot_nt(a, b):
    return lax.dot_general(a, b, (((1,), (1,)), ((), ())), preferred_element_type=F32)


def fetch(pairs, sems):
    copies = [pltpu.make_async_copy(src, dst, sems.at[i]) for i, (src, dst) in enumerate(pairs)]
    for copy in copies:
        copy.start()
    return copies


def lane_iota(shape):
    return lax.broadcasted_iota(I32, shape, len(shape) - 1)


def row_iota(shape):
    return lax.broadcasted_iota(I32, shape, 0)


def roll(x, shift, axis):
    shift = shift % x.shape[axis]
    return x if shift == 0 else pltpu.roll(x, shift, axis)


def lane_gather(row, index):
    return jnp.take_along_axis(jnp.broadcast_to(row, index.shape), index, axis=1)


def host_split(x):
    hi = np.asarray(x, np.float32).astype(BF16)
    lo = (np.asarray(x, np.float64) - hi.astype(np.float64)).astype(BF16)
    return hi, lo


def filter_tables(block_rows):
    turn = 2.0 * math.pi / PATCH
    step = np.arange(PATCH)
    cosine = np.cos(turn * (step[:, None] * step[None, :] % PATCH))
    sine = np.sin(turn * (step[:, None] * step[None, :] % PATCH))
    count = block_rows * PATCH
    az = np.zeros((2 * PATCH, 2 * HALF))
    az[:PATCH, :HALF], az[:PATCH, HALF:] = cosine[:, :HALF], sine[:, :HALF]
    az[PATCH:, :HALF], az[PATCH:, HALF:] = -sine[:, :HALF], cosine[:, :HALF]
    rg = np.zeros((2 * LANES, 4 * PATCH))
    for p in range(2):
        w, wi = slice(p * HALF, p * HALF + PATCH), slice(LANES + p * HALF, LANES + p * HALF + PATCH)
        lr, li = slice(p * PATCH, (p + 1) * PATCH), slice(LANES + p * PATCH, LANES + (p + 1) * PATCH)
        rg[w, lr], rg[wi, lr] = cosine, sine
        rg[w, li], rg[wi, li] = -sine, cosine
    looks = STEP // LOOK
    core = cosine[RIM : RIM + STEP].reshape(looks, LOOK, PATCH).mean(axis=1)
    core_s = sine[RIM : RIM + STEP].reshape(looks, LOOK, PATCH).mean(axis=1)
    back = np.zeros((2 * block_rows * looks, count))
    for u in range(block_rows):
        k = slice(u * PATCH, (u + 1) * PATCH)
        back[u * looks : (u + 1) * looks, k] = core / PATCH
        back[(block_rows + u) * looks : (block_rows + u + 1) * looks, k] = core_s / PATCH
    c_l, s_l = core.T / PATCH, core_s.T / PATCH
    reps = LANES // looks
    patch_of = np.arange(LANES) // looks % 2
    last = np.zeros((4 * LANES, 2 * LANES))
    terms = ((c_l, s_l), (-s_l, c_l), (-s_l, c_l), (-c_l, -s_l))
    for i, (re, im) in enumerate(terms):
        for p in range(2):
            k = slice(i * LANES + p * PATCH, i * LANES + (p + 1) * PATCH)
            last[k, :LANES] = np.tile(re, reps) * (patch_of == p)
            last[k, LANES:] = np.tile(im, reps) * (patch_of == p)
    return az, rg, back, last


def slice_kernel(width, dem_ref, list_ref, out_ref):
    tiles = out_ref.shape[0]
    lats, lons, _ = dem_ref.shape
    packed = LANES // width
    groups = lats // packed
    slots = list_ref.shape[1]
    lane = lane_iota((lons, LANES))
    listed = list_ref[...].astype(F32)
    for q in range(tiles):
        tile, offset = divmod(q * width, LANES)
        for g in range(groups):
            total = None
            for p in range(packed):
                x = dem_ref[p * groups + g, :, tile * LANES : (tile + 1) * LANES]
                x = roll(x, p * width - offset, 1)
                total = x if total is None else jnp.where(lane // width == p, x, total)
            for i in range(lons // QUAD):
                out_ref[q, g * (lons // QUAD) + i] = total[i * QUAD : (i + 1) * QUAD]
        out_ref[q, groups * lons // QUAD, 0:1, 0:slots] = listed


def halo_kernel(par_ref, image_ref, factor_ref, position_ref, one_ref, two_ref):
    even = par_ref[0] == 0
    lines = factor_ref.shape[0]
    fields = (
        lambda s: image_ref[0, s, :],
        lambda s: image_ref[1, s, :],
        lambda s: factor_ref[s, :],
        lambda s: position_ref[s, :].astype(F32),
    )
    for i, field in enumerate(fields):
        first = field(slice(0, RIM))
        last = field(slice(lines - RIM, lines))
        one_ref[i] = jnp.where(even, last, first)
        two_ref[i] = jnp.where(even, first, last)


def border_sums(n_rg, tiles, values, owner_ref, base_ref, share_ref, w_ref, term_ref, col_ref, here_ref, next_ref):
    channels = len(values)
    height, width = owner_ref.shape
    base = base_ref[...]
    last_line = jnp.right_shift(base, width.bit_length() - 1) == height - 1
    last_column = jnp.bitwise_and(base, width - 1) == width - 1
    owner = owner_ref[...]
    on_line = jnp.where(last_line, owner, -1)
    on_column = jnp.where(last_column, owner, -1)
    terms = []
    for c, value in enumerate(values):
        for i in range(2):
            spot = (i * channels + c) * tiles
            far = 4 * channels * tiles + spot
            for mask, k, row in ((0, 2, 2 * spot), (0, 3, 2 * spot + tiles), (1, 1, far), (1, 3, far + 2 * channels * tiles)):
                x = share_ref[k] if value is None else share_ref[k] * value
                high = x.astype(BF16).astype(F32)
                term_ref[len(terms)] = high if i == 0 else x - high
                terms.append((mask, row))
    tile = row_iota((tiles, width))
    for m in range(height):
        cut = slice(m * width, (m + 1) * width)
        masks = (tile == on_line[m : m + 1], tile == on_column[m : m + 1])
        for n, (mask, row) in enumerate(terms):
            w_ref[row : row + tiles, cut] = jnp.where(masks[mask], term_ref[n, m : m + 1, :], 0.0).astype(BF16)
    size = channels * tiles
    b = dot_nt(w_ref[0 : 4 * size], col_ref[...])
    b = b[: 2 * size] + b[2 * size :]
    side = dot_nt(w_ref[4 * size : 6 * size], here_ref[...]) + dot_nt(w_ref[6 * size : 8 * size], next_ref[...])
    side = side[:size] + side[size:]
    results = []
    for c in range(channels):
        b0, b1 = b[2 * c * tiles : (2 * c + 1) * tiles], b[(2 * c + 1) * tiles : (2 * c + 2) * tiles]
        dest = row_iota(b0.shape)
        shifted = roll(b1, 1, 1)
        below = roll(b0, n_rg, 0)
        beside = roll(shifted, n_rg, 0)
        diagonal = jnp.where(dest % n_rg > 0, roll(shifted, n_rg + 1, 0), 0.0)
        beside = jnp.where(lane_iota(b0.shape) == 0, diagonal, beside)
        rows = jnp.where(dest >= n_rg, below + beside, 0.0)
        one = side[c * tiles : (c + 1) * tiles]
        one = jnp.concatenate([jnp.zeros((1, one.shape[1]), F32), one[:-1]], axis=0)
        results.append((rows, jnp.where(row_iota(one.shape) % n_rg > 0, one, 0.0)))
    return results


def add_edges(total, edges, channel, first):
    rows, lanes = row_iota(total.shape), lane_iota(total.shape)
    edge, side = edges[first + channel : first + channel + 1], edges[first + 3 : first + 4]
    column = jnp.sum(jnp.where(lanes == rows + channel * total.shape[0], side, 0.0), axis=1, keepdims=True)
    return total + jnp.where(rows == 0, edge, 0.0) + jnp.where(lanes == 0, column, 0.0)


def pack_kernel(n_rg, cap_rows, owner_ref, base_ref, share_ref, early_ref, cell_ref, rim_ref, side_ref, im_ref, in_ref, col_ref, here_ref, next_ref, hot_ref, lhs_ref, w_ref, term_ref):
    tiles = early_ref.shape[0]
    height, width = owner_ref.shape
    owner = owner_ref[...]
    batch = min(tiles, 16)
    tri = (row_iota((width, width)) < lane_iota((width, width))).astype(BF16)
    ones = jnp.ones((width, width), BF16)
    size = batch * height
    r, c = row_iota((size, size)), lane_iota((size, size))
    lower = ((r // height == c // height) & (c < r)).astype(BF16)
    rank = jnp.zeros((height, width), F32)
    for b in range(tiles // batch):
        hot = jnp.concatenate([(owner == b * batch + o).astype(F32) for o in range(batch)], axis=0)
        hot16 = hot.astype(BF16)
        before = dot(hot16, tri) + dot(lower, dot(hot16, ones).astype(BF16))
        kept = hot * before
        for o in range(batch):
            rank = rank + kept[o * height : (o + 1) * height]
    rank = rank.astype(I32)
    base = base_ref[...]
    shift = width.bit_length() - 1
    column = jnp.bitwise_and(base, width - 1)
    line = jnp.right_shift(base, shift)
    cap = cap_rows * LANES
    for m in range(height):
        cut = slice(m * width, (m + 1) * width)
        hot_ref[:, cut] = (row_iota((cap, width)) == rank[m : m + 1]).astype(F32).astype(BF16)
        col_ref[:, cut] = (row_iota((width, width)) == column[m : m + 1]).astype(F32).astype(BF16)
        mine = row_iota((tiles, width)) == owner[m : m + 1]
        lhs_ref[0:tiles, cut] = mine.astype(F32).astype(BF16)
        lhs_ref[tiles : 2 * tiles, cut] = jnp.where(mine, float(m), 0.0).astype(BF16)
        lhs_ref[2 * tiles :, cut] = jnp.where(mine, lane_iota((tiles, width)).astype(F32), 0.0).astype(BF16)
        at = row_iota((height, width))
        here_ref[:, cut] = (at == line[m : m + 1]).astype(F32).astype(BF16)
        next_ref[:, cut] = (at == line[m : m + 1] + 1).astype(F32).astype(BF16)
    found = dot_nt(lhs_ref[...], hot_ref[...])
    valid = found[0:tiles] > 0.5
    at_m = found[tiles : 2 * tiles].astype(I32)
    at_n = found[2 * tiles :].astype(I32)
    im_ref[...] = at_m
    in_ref[...] = at_n
    cell = base.astype(F32)
    for channel in range(5):
        for k in range(cap_rows):
            cut = slice(k * LANES, (k + 1) * LANES)
            total = jnp.zeros((tiles, LANES), F32)
            for m in range(height):
                row = cell[m : m + 1] if channel == 4 else share_ref[channel, m : m + 1, :]
                total = jnp.where(at_m[:, cut] == m, lane_gather(row, at_n[:, cut]), total)
            total = jnp.where(valid[:, cut], total, 0.0)
            if channel == 4:
                cell_ref[:, cut] = total
            else:
                early_ref[:, channel * cap_rows + k, :] = total
    ((rows, side),) = border_sums(n_rg, tiles, [None], owner_ref, base_ref, share_ref, w_ref, term_ref, col_ref, here_ref, next_ref)
    rim_ref[...] = rows
    side_ref[...] = side


def request_kernel(n_rg, grid, width, table_rows, slots, got_ref, early_ref, cell_ref, out_ref, turn_ref, list_ref, index_ref, sem):
    tiles, quads = got_ref.shape[:2]
    rows = (quads - 1) * QUAD
    lats, lons = grid
    packed = LANES // width
    groups = lats // packed
    listed = jnp.concatenate([got_ref[t, quads - 1, 0:1, :] for t in range(tiles)], axis=0)
    listed = jnp.maximum(listed, 0.0)
    listed = jnp.where(lane_iota(listed.shape) < slots, listed, 0.0).astype(I32)
    lat, lon = listed // (lons * n_rg), listed % (lons * n_rg)
    key = lat // lats * n_rg + lon // lons
    row, piece = key * rows + lat % lats % groups * lons + lon % lons, lat % lats // groups
    for place in range(packed):
        list_ref[place] = jnp.bitwise_and(place - piece, packed - 1) * (tiles * rows) + row
    (copy,) = fetch(((list_ref, index_ref),), sem)
    for t in range(tiles):
        for i in range(rows // QUAD):
            turn_ref[t * rows + i * QUAD : t * rows + (i + 1) * QUAD, :] = got_ref[t, i]
        x = turn_ref[t * rows : (t + 1) * rows, :]
        for p in range(1, packed):
            at = (p * tiles + t) * rows
            turn_ref[at : at + rows, :] = roll(x, p * width, 1)
        out_ref[t, table_rows:, :] = early_ref[t]
        if t < n_rg or t >= tiles - n_rg:
            out_ref[t, 0:table_rows, :] = jnp.zeros((table_rows, LANES), F32)
    for k in range(cell_ref.shape[1] // LANES):
        x = cell_ref[:, k * LANES : (k + 1) * LANES]
        for i in range(packed):
            place, line = divmod(3 * slots + k * packed + i, table_rows)
            cut = slice(place * width, (place + 1) * width)
            out_ref[:, line, cut] = roll(x, (place - i) * width, 1)[:, cut]
    copy.wait()
    for t in range(tiles):
        for f in range(slots):
            found = {}
            for n, dest in ((0, t + n_rg), (1, t), (2, t - n_rg)):
                if 0 <= dest < tiles:
                    place, line = divmod(n * slots + f, table_rows)
                    if place not in found:
                        found[place] = turn_ref[pl.ds(index_ref[place, t, f], 1), :]
                    cut = slice(place * width, (place + 1) * width)
                    out_ref[dest, line : line + 1, cut] = found[place][:, cut]


def sincos(x):
    n = jnp.floor(x * (2.0 / math.pi) + 0.5)
    r = x - n * 1.5703125
    r = r - n * 4.837512969970703e-4
    r = r - n * 7.549789954891882e-8
    z = r * r
    s = ((-1.9515295891e-4 * z + 8.3321608736e-3) * z - 1.6666654611e-1) * z * r + r
    c = ((2.443315711809948e-5 * z - 1.388731625493765e-3) * z + 4.166664568298827e-2) * z * z - 0.5 * z + 1.0
    q = n.astype(I32)
    odd = (q & 1) == 1
    sine = jnp.where(odd, c, s)
    cosine = jnp.where(odd, s, c)
    sine = jnp.where((q & 2) == 2, -sine, sine)
    cosine = jnp.where(((q + 1) & 2) == 2, -cosine, cosine)
    return cosine, sine


def flatten_kernel(width, table_rows, slots, par_ref, got_ref, image_ref, factor_ref, position_ref, one_ref, two_ref, flat_ref, edge_ref, tab_ref):
    even = par_ref[0] == 0
    lines, samples = factor_ref.shape
    packed = LANES // width
    tiles = got_ref.shape[0]
    parts = tiles // packed
    lane = lane_iota((table_rows, LANES))
    for k in range(parts):
        for place in range(packed):
            total = None
            for j in range(packed):
                x = roll(got_ref[k * packed + j, 0:table_rows, :], (j - place) * width, 1)
                total = x if total is None else jnp.where(lane // width == j, x, total)
            tab_ref[k, place * table_rows : (place + 1) * table_rows, :] = total
    cols = samples // LANES
    shift = LANES.bit_length() - 1
    part_bits = parts.bit_length() - 1
    own = (lambda c: (lambda spot: image_ref[(c, *spot)]))

    def rim_field(n, below):
        def read(spot):
            a, b = one_ref[(n, *spot)], two_ref[(n, *spot)]
            return jnp.where(even, a, b) if below else jnp.where(even, b, a)

        return read

    fields = [own(0), own(1), lambda spot: factor_ref[spot], lambda spot: position_ref[spot]]
    strips = [(0, [rim_field(n, False) for n in range(4)], RIM), (1, fields, lines), (2, [rim_field(n, True) for n in range(4)], RIM)]
    line = 0
    for table, sources, height in strips:
        for start in range(0, height, 8):
            for c in range(cols):
                spot = (slice(start, start + 8), slice(c * LANES, (c + 1) * LANES))
                re, im, factor, at = [read(spot) for read in sources]
                at = at.astype(I32)
                lanes = jnp.bitwise_and(at, LANES - 1)
                bits = [jnp.bitwise_and(at, LANES << b) != 0 for b in range(part_bits)]
                slot = jnp.right_shift(at, shift + part_bits)
                found = None
                for f in range(slots):
                    row = table * slots + f
                    x = [
                        jnp.take_along_axis(jnp.broadcast_to(tab_ref[k, row : row + 1, :], (8, LANES)), lanes, axis=1)
                        for k in range(parts)
                    ]
                    for bit in bits:
                        x = [jnp.where(bit, x[n + 1], x[n]) for n in range(0, len(x), 2)]
                    found = x[0] if f == 0 else jnp.where(slot == f, x[0], found)
                cosine, sine = sincos(factor * found)
                flat_ref[0, line : line + 8, spot[1]] = re * cosine + im * sine
                flat_ref[1, line : line + 8, spot[1]] = im * cosine - re * sine
            line += 8
    edge = lane_iota((lines + 2 * RIM, LANES))
    for c in range(2):
        first = flat_ref[c, :, 0:LANES]
        last = roll(flat_ref[c, :, samples - LANES : samples], 2 * RIM, 1)
        edge_ref[c] = jnp.where(edge < RIM, first, jnp.where(edge < 2 * RIM, last, 0.0))


def root(x):
    return x * lax.rsqrt(jnp.maximum(x, 1e-37))


def stack_parts(x_ref, c, at, x):
    high, low = split(x)
    x_ref[c * HALF : (c + 1) * HALF, at] = high
    x_ref[(2 + c) * HALF : (3 + c) * HALF, at] = low
    x_ref[(4 + c) * HALF : (5 + c) * HALF, at] = high


def spectrum(strips):
    flip = jnp.where(row_iota(strips[0].shape) % 2 == 0, 1.0, -1.0)
    return jnp.concatenate([one + flip * two for one, two in zip(strips[:-1], strips[1:])], axis=0)


def range_dft(windows, const_ref):
    (rh, rl), (ih, il) = [split(jnp.concatenate(x, axis=0)) for x in windows]
    size = 2 * LANES
    main, rest = const_ref[:size], const_ref[size : 2 * size]
    return dot(jnp.concatenate([rh, ih, rl, il, rh, ih], axis=1), jnp.concatenate([main, main, rest], axis=0))


def transform_kernel(flat_ref, az_ref, const_ref, out_ref, x_ref):
    _, rows, samples = flat_ref.shape
    cols = samples // LANES
    wide = (cols + 1) * LANES
    lane = lane_iota((HALF, LANES))
    for p in range(rows // HALF):
        for c in range(2):
            before = 0.0
            for j in range(cols + 1):
                now = 0.0
                if j < cols:
                    now = roll(flat_ref[c, p * HALF : (p + 1) * HALF, j * LANES : (j + 1) * LANES], RIM, 1)
                at = slice(p * wide + j * LANES, p * wide + (j + 1) * LANES)
                stack_parts(x_ref, c, at, jnp.where(lane < RIM, before, now))
                before = now
    e = dot(az_ref[...], x_ref[...])
    windows = []
    for c in range(2):
        cut = slice(c * PATCH, (c + 1) * PATCH)
        cells = [
            spectrum([e[cut, p * wide + j * LANES : p * wide + (j + 1) * LANES] for p in range(rows // HALF)])
            for j in range(cols + 1)
        ]
        half = lane_iota(cells[0].shape) < PATCH
        turned = [pltpu.roll(x, PATCH, 1) for x in cells]
        found = []
        for j in range(cols):
            found += [cells[j], jnp.where(half, turned[j], turned[j + 1])]
        windows.append(found)
    out_ref[...] = range_dft(windows, const_ref)


def filter_kernel(n_rg, cap_rows, block_rows, rg_ref, y_ref, edge_ref, rim_ref, side_ref, im_ref, in_ref, owner_ref, base_ref, share_ref, az_ref, const_ref, col_ref, here_ref, next_ref, out_ref, x_ref, rim_y_ref, m_ref, s_ref, p_ref, z_ref, look_ref, w_ref, term_ref):
    strips = edge_ref.shape[1] // HALF
    lane = lane_iota((HALF, LANES))
    left = rg_ref[0] > 0
    right = rg_ref[0] < n_rg - 1
    for p in range(strips):
        for c in range(2):
            halo = edge_ref[c, p * HALF : (p + 1) * HALF]
            before = jnp.where(left, roll(halo, -RIM, 1), 0.0)
            after = jnp.where(right & (lane < 2 * RIM), roll(halo, RIM, 1), 0.0)
            stack_parts(x_ref, c, slice(p * LANES, (p + 1) * LANES), jnp.where(lane < RIM, before, after))
    looks = block_rows * STEP // LOOK
    block = const_ref[...]

    def tripled(at, size):
        return jnp.concatenate([block[at : at + size], block[at : at + size], block[at + size : at + 2 * size]], axis=0)

    last3 = tripled(4 * LANES, 4 * LANES)
    near = jnp.concatenate([block[12 * LANES : 13 * LANES, :LANES]] * 2, axis=0)
    side = jnp.concatenate([block[12 * LANES : 13 * LANES, LANES:]] * 2, axis=0)
    back = block[13 * LANES : 13 * LANES + 4 * looks, : 2 * block_rows * PATCH]
    rim = dot(az_ref[...], x_ref[...])
    count = block_rows * PATCH
    pairs = y_ref.shape[0] // count
    windows = []
    for c in range(2):
        x = spectrum([rim[c * PATCH : (c + 1) * PATCH, p * LANES : (p + 1) * LANES] for p in range(strips)])
        first = lane_iota(x.shape) < RIM
        windows.append([jnp.where(first, x, 0.0), pltpu.roll(jnp.where(first, 0.0, x), PATCH, 1)])
    rim_y_ref[...] = range_dft(windows, const_ref)
    rim_y_ref[:count] = rim_y_ref[:count] + y_ref[:count]
    rim_y_ref[count:] = rim_y_ref[count:] + y_ref[(pairs - 1) * count :]

    def everywhere(step):
        step(0, rim_y_ref, 0)
        pl.loop(1, pairs - 1, unroll=pairs - 2)(lambda w: step(w, y_ref, w))
        step(pairs - 1, rim_y_ref, 1)

    def measure(w, ref, place):
        at = pl.multiple_of(w * count, count)
        cut = pl.ds(pl.multiple_of(place * count, count), count)
        re, im = ref[cut, :LANES], ref[cut, LANES:]
        magnitude = root(re * re + im * im)
        high, low = split(magnitude)
        m_ref[pl.ds(at, count), :LANES] = high
        m_ref[pl.ds(at, count), LANES:] = low
        for u in range(block_rows):
            part = magnitude[u * PATCH : u * PATCH + 8]
            for i in range(1, PATCH // 8):
                part = part + magnitude[u * PATCH + 8 * i : u * PATCH + 8 * i + 8]
            p_ref[pl.ds(pl.multiple_of((w * block_rows + u) * 8, 8), 8), :] = part

    everywhere(measure)
    s_ref[...] = dot(m_ref[...], near)
    ph, plow = split(p_ref[...])
    sums = dot(jnp.concatenate([ph, plow], axis=1), side)
    for n in range(pairs * block_rows):
        x = sums[8 * n : 8 * n + 8]
        for shift in (4, 2, 1):
            x = x + pltpu.roll(x, shift, 0)
        p_ref[8 * n : 8 * n + 8, :] = 1.0 / (9.0 * (x * (1.0 / (PATCH * PATCH)) + EPS))

    def weigh(w, ref, place):
        at = pl.multiple_of(w * 2 * LANES, 2 * LANES)
        for u in range(block_rows):
            cut = pl.ds(pl.multiple_of(w * count + u * PATCH, PATCH), PATCH)
            su = s_ref[cut, :]
            su = su + pltpu.roll(su, 1, 0) + pltpu.roll(su, PATCH - 1, 0)
            factor = p_ref[pl.ds(pl.multiple_of((w * block_rows + u) * 8, 8), 8), :]
            gain = root(su * jnp.concatenate([factor] * (PATCH // 8), axis=0))
            for c in range(2):
                source = pl.ds(pl.multiple_of(place * count + u * PATCH, PATCH), PATCH)
                high, low = split(ref[source, c * LANES : (c + 1) * LANES] * gain)
                span = pl.ds(pl.multiple_of(at + c * LANES, LANES), LANES)
                z_ref[u * PATCH : (u + 1) * PATCH, span] = high
                z_ref[count + u * PATCH : count + (u + 1) * PATCH, span] = low

    everywhere(weigh)
    t = dot(back, z_ref[...])
    t = t[: 2 * looks] + t[2 * looks :]
    stacked = jnp.concatenate(
        [
            jnp.concatenate([t[i * looks : (i + 1) * looks, w * 2 * LANES : (w + 1) * 2 * LANES] for i in range(2)], axis=1)
            for w in range(pairs)
        ],
        axis=0,
    )
    sh, sl = split(stacked)
    y = dot(jnp.concatenate([sh, sl, sh], axis=1), last3)
    group = lane_iota((looks, LANES)) // (2 * STEP // LOOK)
    for c in range(2):
        total = jnp.zeros((looks, LANES), F32)
        for w in range(pairs):
            total = jnp.where(group == w, y[w * looks : (w + 1) * looks, c * LANES : (c + 1) * LANES], total)
        look_ref[c] = total
    tiles = out_ref.shape[0]
    for k in range(cap_rows):
        cut = slice(k * LANES, (k + 1) * LANES)
        at_m, at_n = im_ref[:, cut], in_ref[:, cut]
        for c in range(2):
            total = jnp.zeros((tiles, LANES), F32)
            for m in range(looks):
                total = jnp.where(at_m == m, lane_gather(look_ref[c, m : m + 1, :], at_n), total)
            out_ref[:, c * cap_rows + k, :] = total
    values = [look_ref[0], look_ref[1]]
    borders = border_sums(n_rg, tiles, values, owner_ref, base_ref, share_ref, w_ref, term_ref, col_ref, here_ref, next_ref)
    for c, (rows, side) in enumerate(borders):
        out_ref[:, 2 * cap_rows + c, :] = rows
        out_ref[:, 2 * cap_rows + 3, c * looks : (c + 1) * looks] = side
    out_ref[:, 2 * cap_rows + 2, :] = rim_ref[...]
    out_ref[:, 2 * cap_rows + 3, 2 * looks : 3 * looks] = side_ref[...]


def prepare_kernel(cap_rows, table_rows, slots, width, map_lat, got_ref, hot_ref, row_ref, sum_ref):
    tiles = got_ref.shape[0]
    packed = LANES // width
    lane = lane_iota((1, LANES))
    for t in range(tiles):
        for k in range(cap_rows):
            def channel(c):
                return got_ref[t, table_rows + c * cap_rows + k : table_rows + c * cap_rows + k + 1, :]

            cell = None
            for i in range(packed):
                place, spot = divmod(3 * slots + k * packed + i, table_rows)
                x = roll(got_ref[t, spot : spot + 1, :], (i - place) * width, 1)
                cell = x if cell is None else jnp.where(lane // width == i, x, cell)
            cell = cell.astype(I32)
            line, column = jnp.right_shift(cell, LANES.bit_length() - 1), jnp.bitwise_and(cell, LANES - 1)
            at = (t * cap_rows + k) * LANES
            cut = slice(at, at + LANES)
            hot_ref[:, cut] = (row_iota((LANES, LANES)) == column).astype(F32).astype(BF16)
            rows = row_iota((map_lat, LANES))
            here, next_line = rows == line, rows == line + 1
            for d in range(2):
                row_ref[d * map_lat : (d + 1) * map_lat, cut] = jnp.where(here, channel(d), 0.0) + jnp.where(
                    next_line, channel(2 + d), 0.0
                )
    high, low = split(row_ref[...])
    acc = dot_nt(high, hot_ref[...]) + dot_nt(low, hot_ref[...])
    shifted = roll(acc[map_lat:], 1, 1)
    total = acc[:map_lat] + jnp.where(lane_iota(shifted.shape) == 0, 0.0, shifted)
    sum_ref[...] = total


def splat_kernel(cap_rows, map_lat, got_ref, hot_ref, row_ref, weight_ref, out_ref, x_ref):
    tiles = got_ref.shape[0]
    wide = 2 * map_lat
    for t in range(tiles):
        for k in range(cap_rows):
            cut = slice((t * cap_rows + k) * LANES, (t * cap_rows + k + 1) * LANES)
            for c in range(2):
                value = got_ref[t, c * cap_rows + k : c * cap_rows + k + 1, :]
                high, low = split(row_ref[:, cut] * value)
                x_ref[c * wide : (c + 1) * wide, cut] = high
                x_ref[(2 + c) * wide : (3 + c) * wide, cut] = low
    acc = dot_nt(x_ref[...], hot_ref[...])
    acc = acc[: 2 * wide] + acc[2 * wide :]
    edges = got_ref[0]
    for t in range(1, tiles):
        edges = edges + got_ref[t]
    weight = jnp.maximum(add_edges(weight_ref[...], edges, 2, 2 * cap_rows), 1.0)
    for c in range(2):
        shifted = roll(acc[c * wide + map_lat : (c + 1) * wide], 1, 1)
        total = acc[c * wide : c * wide + map_lat] + jnp.where(lane_iota(shifted.shape) == 0, 0.0, shifted)
        out_ref[c] = add_edges(total, edges, c, 2 * cap_rows) / weight


def filter_constants(block_rows):
    az, rg, back, last = filter_tables(block_rows)
    az_h, az_l = host_split(az)
    rg_h, rg_l = host_split(rg)
    back_h, back_l = host_split(back)
    last_h, last_l = host_split(last)
    zero = np.zeros_like(back_l)
    lane = np.arange(LANES)
    same = lane[:, None] // PATCH == lane[None, :] // PATCH
    apart = (lane[:, None] - lane[None, :]) % PATCH
    near = (same & ((apart <= 1) | (apart == PATCH - 1))).astype(BF16)
    blocks = (
        np.concatenate([rg_h, rg_l], axis=0),
        np.concatenate([last_h, last_l], axis=0),
        np.concatenate([near, same.astype(BF16)], axis=1),
        np.concatenate([np.concatenate([back_h, back_h], axis=1), np.concatenate([back_l, zero], axis=1)], axis=0),
    )
    wide = [np.pad(b, ((0, 0), (0, 2 * LANES - b.shape[1]))) for b in blocks]
    return np.concatenate([az_h, az_h, az_l], axis=1), np.concatenate(wide, axis=0)


def filter_scratch(rows, samples, block_rows, map_lat, map_lon, tiles):
    patches = samples // STEP
    count = block_rows * PATCH
    return (
        VMEM((6 * HALF, rows // HALF * LANES), BF16),
        VMEM((2 * count, 2 * LANES), F32),
        VMEM((patches // 2 * count, 2 * LANES), BF16),
        VMEM((patches // 2 * count, LANES), F32),
        VMEM((patches // 2 * block_rows * 8, LANES), F32),
        VMEM((2 * count, patches * LANES), BF16),
        VMEM((2, map_lat, map_lon), F32),
        VMEM((16 * tiles, map_lat * map_lon), BF16),
        VMEM((16, map_lat, map_lon), F32),
    )


def swap_pairs(count, first):
    return [p for i in range(first, count - 1, 2) for p in ((i, i + 1), (i + 1, i))]


def scene(image, factor, heights, listing, position, owner, base, shares):
    n_az, n_rg = lax.axis_size("az"), lax.axis_size("rg")
    tiles = n_az * n_rg
    both = ("az", "rg")
    lats, lons, points = heights.shape
    slots = listing.shape[1]
    width = points // tiles
    packed = LANES // width
    lines, samples = factor.shape
    map_lat, map_lon = lines // LOOK, samples // LOOK
    block_rows = lines // STEP
    capacity = 2 * map_lat * map_lon // tiles
    cap_rows = -(-capacity // LANES)
    table_rows = -(-(3 * slots + cap_rows * packed) // packed)
    table_rows = -(-table_rows // 8) * 8
    early_rows = 4 * cap_rows
    late_rows = -(-(2 * cap_rows + 4) // 8) * 8
    slice_rows = lats * lons // packed
    parity = (lax.axis_index("az") % 2).astype(I32).reshape(1)
    rg = lax.axis_index("rg").astype(I32).reshape(1)

    def exchange(x):
        return lax.all_to_all(x, both, split_axis=0, concat_axis=0, tiled=True)

    slices = call(
        functools.partial(slice_kernel, width),
        sds((tiles, slice_rows // QUAD + 1, QUAD, LANES)),
        (heights, listing),
        grant=60,
    )
    got_slices = exchange(slices)
    one, two = call(halo_kernel, [sds((4, RIM, samples))] * 2, (parity, image, factor, position), smem=(0,))
    one = lax.ppermute(one, "az", swap_pairs(n_az, 0))
    two = lax.ppermute(two, "az", swap_pairs(n_az, 1))
    total = map_lat * map_lon
    looks_at = (owner.reshape(map_lat, map_lon), base.reshape(map_lat, map_lon), shares.reshape(4, map_lat, map_lon))
    early, cells, rim_sum, side_sum, at_m, at_n, *edges = call(
        functools.partial(pack_kernel, n_rg, cap_rows),
        [
            sds((tiles, early_rows, LANES)),
            sds((tiles, cap_rows * LANES)),
            sds((tiles, map_lon)),
            sds((tiles, map_lat)),
            sds((tiles, cap_rows * LANES), I32),
            sds((tiles, cap_rows * LANES), I32),
            sds((map_lon, total), BF16),
            sds((map_lat, total), BF16),
            sds((map_lat, total), BF16),
        ],
        looks_at,
        scratch=(VMEM((cap_rows * LANES, total), BF16), VMEM((3 * tiles, total), BF16), VMEM((8 * tiles, total), BF16), VMEM((8, map_lat, map_lon), F32)),
    )
    request = call(
        functools.partial(request_kernel, n_rg, (lats, lons), width, table_rows, slots),
        sds((tiles, table_rows + early_rows, LANES)),
        (got_slices, early, cells),
        scratch=(
            VMEM((packed * tiles * slice_rows, LANES), F32),
            VMEM((packed, tiles, LANES), I32),
            pltpu.SMEM((packed, tiles, LANES), I32),
            pltpu.SemaphoreType.DMA((1,)),
        ),
    )
    tables = exchange(request)
    flat, edge = call(
        functools.partial(flatten_kernel, width, table_rows, slots),
        [sds((2, lines + 2 * RIM, samples)), sds((2, lines + 2 * RIM, LANES))],
        (parity, tables, image, factor, position, one, two),
        smem=(0,),
        scratch=(
            VMEM((tiles // packed, packed * table_rows, LANES), F32),
        ),
    )
    edge = lax.ppermute(edge, "rg", swap_pairs(n_rg, 0))
    az_parts, constants = filter_constants(block_rows)
    wide = (lines + 2 * RIM) // HALF * (samples + LANES)
    patches = samples // STEP
    count = block_rows * PATCH
    lines_done = call(
        transform_kernel,
        sds((patches // 2 * count, 2 * LANES)),
        (flat, az_parts, constants),
        scratch=(VMEM((6 * HALF, wide), BF16),),
    )
    rows = lines + 2 * RIM
    patches = samples // STEP
    count = block_rows * PATCH
    packed_looks = call(
        functools.partial(filter_kernel, n_rg, cap_rows, block_rows),
        sds((tiles, late_rows, LANES)),
        (rg, lines_done, edge, rim_sum, side_sum, at_m, at_n, *looks_at, az_parts, constants, *edges),
        smem=(0,),
        scratch=filter_scratch(rows, samples, block_rows, map_lat, map_lon, tiles),
    )
    got = exchange(packed_looks)
    wide = tiles * cap_rows * LANES
    hot, row_weights, weight_sum = call(
        functools.partial(prepare_kernel, cap_rows, table_rows, slots, width, map_lat),
        [sds((LANES, wide), BF16), sds((2 * map_lat, wide)), sds((map_lat, map_lon))],
        (tables,),
    )
    return call(
        functools.partial(splat_kernel, cap_rows, map_lat),
        sds((2, map_lat, map_lon)),
        (got, hot, row_weights, weight_sum),
        scratch=(VMEM((8 * map_lat, wide), BF16),),
    )


def solution(mesh):
    return jax.shard_map(
        scene,
        mesh=mesh,
        in_specs=(
            P(None, ("scene", "az"), "rg"),
            P(("scene", "az"), "rg"),
            P(("scene", "az"), "rg", None),
            P(("scene", "az", "rg"), None),
            P(("scene", "az"), "rg"),
            P(("scene", "az", "rg"), None),
            P(("scene", "az", "rg")),
            P(None, ("scene", "az", "rg")),
        ),
        out_specs=P(None, ("scene", "az"), "rg"),
        check_vma=False,
    )
```
